768 devices in a mesh: band: 48 (over x, z), fld: 16 (over y, core).
Axes of the slice: x: 4, y: 8, z: 12, core: 2. Of those that a mesh axis runs over, the one named last changes fastest.
Arguments:
- grid_fields: bfloat16 [32, 2, 768, 3072], P('fld', None, 'band'), may hold values from -6 to 6
- legendre: bfloat16 [768, 2, 768, 513], P(('band', 'fld')), may hold values from -0.21875 to 0.21875
- slot_wave: int32 [1536], P(('band', 'fld')), may hold values from 0 to 1024, as said below
Outputs:
- spectrum: bfloat16 [768, 2, 32, 2, 513], P(('band', 'fld'))
The draws below stay inside these ranges and needn't reach their ends.
Inputs may be any that keep to these rules, and one draw needn't show every extreme that they name: `slot_wave`: for every q, slots 2 q and 2 q + 1 hold m and 1023 - m for some m below 512, or both hold 1024; every wavenumber below 1024 is held by exactly one slot.
All inputs are finite; a program needn't handle non-finite values.
Results may differ from the reference program's by a relative error of at most 0.0059.
Values may be sent and summed in bfloat16 or wider, within the bound.
A program may use at most 32 MiB of HBM per device.

```python
import math
import jax
import jax.numpy as jnp
from jax import lax

NLON = 3072
HALF = 768
MM = 1024
FL = 32
SLOTS = 1536
PAIRS = 768
HCOL = 513


def draw_slot_wave(key, part):
    pair_slots = SLOTS // 2
    slot_order = jax.random.permutation(jax.random.fold_in(key, 11), pair_slots).astype(jnp.int32)
    half_count = MM // 2
    first_wave = jnp.where(slot_order < half_count, slot_order, MM)
    second_wave = jnp.where(slot_order < half_count, MM - 1 - slot_order, MM)
    return jnp.stack([first_wave, second_wave], axis=1).reshape(SLOTS).astype(jnp.int32)


def steps_of(key, dims, shards, low, high):
    def one(axis_at, blocks):
        heights = jax.random.uniform(jax.random.fold_in(jax.random.fold_in(key, 6), axis_at), (blocks,), jnp.float32, low / len(shards), high / len(shards))
        return jnp.repeat(jnp.exp(heights), dims[axis_at] // blocks).reshape((-1,) + (1,) * (len(dims) - axis_at - 1))

    level = one(*shards[0])
    for cut in shards[1:]:
        level = level * one(*cut)
    return level


def centred(rng, dims, deviation, bound, cuts=(), kind=jnp.bfloat16):
    array = deviation * jax.random.normal(rng, dims, jnp.float32)
    if cuts:
        array = array * steps_of(rng, dims, cuts, -0.22, 0.18)
    return jnp.clip(array, -bound, bound).astype(kind)


def setup_inputs(seed: int = 0) -> dict:
    splits = jax.random.split(jax.random.key(seed), 4)
    return {
        "grid_fields": centred(splits[0], (FL, 2, HALF, NLON), 1.0, 6.0, ((0, 16), (2, 48))),
        "legendre": centred(splits[1], (PAIRS, 2, HALF, HCOL), HALF ** -0.5, 0.21875, ((0, 768),)),
        "slot_wave": draw_slot_wave(jax.random.fold_in(splits[3], 71), 0),
    }


def build_table(wave_list, lon_count):
    lon_index = lax.broadcasted_iota(jnp.int32, (lon_count, wave_list.shape[0]), 0)
    phase_index = lon_index * wave_list[None, :] % lon_count
    phase_angle = phase_index.astype(jnp.float32) * (2.0 * math.pi / lon_count)
    norm_scale = 1.0 / math.sqrt(lon_count)
    live_mask = (wave_list < MM)[None, :]
    cosine = jnp.where(live_mask, jnp.cos(phase_angle) * norm_scale, 0.0)
    sine_part = jnp.where(live_mask, -jnp.sin(phase_angle) * norm_scale, 0.0)
    return jnp.stack([cosine, sine_part], axis=1).astype(jnp.bfloat16)

def reference(grid_fields, legendre, slot_wave):
    fields, hemispheres, half_rows, lon_count = grid_fields.shape
    fourier_table = build_table(jnp.arange(MM, dtype=jnp.int32), lon_count)
    grid_rows = grid_fields.reshape(fields * hemispheres * half_rows, lon_count).astype(jnp.float32)
    flat_table = fourier_table.reshape(lon_count, 2 * MM).astype(jnp.float32)
    fourier = jnp.dot(grid_rows, flat_table, precision=lax.Precision.HIGHEST)
    fourier = fourier.reshape(fields, hemispheres, half_rows, 2, MM)
    north_part = fourier[:, 0]
    south_part = fourier[:, 1]
    folded = jnp.stack([north_part + south_part, north_part - south_part], axis=1).astype(jnp.bfloat16)
    folded = jnp.concatenate([folded, jnp.zeros((fields, 2, half_rows, 2, 1), jnp.bfloat16)], axis=4)
    column = lax.broadcasted_iota(jnp.int32, (2, legendre.shape[3]), 1)
    parity = lax.broadcasted_iota(jnp.int32, (2, legendre.shape[3]), 0)

    def one_pair(pair_args):
        pair_wave, pair_table = pair_args
        columns = jnp.take(folded, pair_wave.astype(jnp.int32), axis=4).astype(jnp.float32)
        products = jnp.einsum('fphrk,phc->pfrkc', columns, pair_table.astype(jnp.float32), precision=lax.Precision.HIGHEST)
        first_count = (MM - pair_wave[0] + 1 - parity) // 2
        second_count = (pair_wave[0] + 2 - parity) // 2
        first_mask = (column < first_count)[:, None, None, :]
        second_mask = ((column >= first_count) & (column < first_count + second_count))[:, None, None, :]
        picked = jnp.where(first_mask, products[:, :, :, 0], jnp.where(second_mask, products[:, :, :, 1], 0.0))
        return picked.astype(jnp.bfloat16)
    return lax.map(one_pair, (slot_wave.reshape(-1, 2), legendre))
```

```python
import math

import jax
import jax.numpy as jnp
import numpy as np
from jax import lax
from jax.experimental import pallas as pl
from jax.experimental.pallas import tpu as pltpu
from jax.sharding import PartitionSpec as P

MM = 1024
NLON = 3072
INNER = 384
BANDS, FLDS = 48, 16
ZS = 12
STEPS = 16


def wave_rows(group, half):
    return group if half == 0 else (4 if group == 0 else 8 - group)


def table_seeds():
    waves = np.zeros((2, 4, 2, 64), np.int64)
    for s in range(2):
        for u in range(4):
            for half in range(2):
                waves[s, u, half] = wave_rows(u, half) + 8 * (64 * s + np.arange(64))
    waves = waves.reshape(1, 1024)
    rows = np.arange(STEPS).reshape(STEPS, 1)
    first = 2.0 * np.pi * ((rows * waves) % NLON) / NLON
    turn = np.broadcast_to(2.0 * np.pi * ((STEPS * waves) % NLON) / NLON, (STEPS, 1024))
    scale = 1.0 / math.sqrt(NLON)
    return np.stack([np.cos(first) * scale, np.sin(first) * scale, np.cos(turn), np.sin(turn)]).astype(np.float32)


def make_table(seeds, table):
    lane = lax.broadcasted_iota(jnp.int32, (STEPS, 128), 1)
    first_half = lane < 64
    for s in range(2):

        def rows(step, carry):
            at = pl.multiple_of(step * STEPS, STEPS)
            after = []
            for u in range(4):
                cosine, sine = carry[u]
                low, high = pl.ds(at, STEPS), pl.ds(at + INNER, STEPS)
                real, imag = pl.ds(s * 256, 128), pl.ds(s * 256 + 128, 128)
                if u == 0:
                    table[u, low, real] = jnp.where(first_half, cosine, 0.0).astype(jnp.bfloat16)
                    table[u, low, imag] = jnp.where(first_half, -sine, 0.0).astype(jnp.bfloat16)
                    table[u, high, real] = jnp.where(first_half, 0.0, cosine).astype(jnp.bfloat16)
                    table[u, high, imag] = jnp.where(first_half, 0.0, -sine).astype(jnp.bfloat16)
                else:
                    table[u, low, real] = cosine.astype(jnp.bfloat16)
                    table[u, low, imag] = (-sine).astype(jnp.bfloat16)
                    table[u, high, real] = jnp.where(first_half, sine, -sine).astype(jnp.bfloat16)
                    table[u, high, imag] = jnp.where(first_half, cosine, -cosine).astype(jnp.bfloat16)
                columns = pl.ds((s * 4 + u) * 128, 128)
                turn_cos, turn_sin = seeds[2, :, columns], seeds[3, :, columns]
                after.append((cosine * turn_cos - sine * turn_sin, sine * turn_cos + cosine * turn_sin))
            return tuple(after)

        start = tuple(
            (seeds[0, :, pl.ds((s * 4 + u) * 128, 128)], seeds[1, :, pl.ds((s * 4 + u) * 128, 128)]) for u in range(4)
        )
        lax.fori_loop(0, INNER // STEPS, rows, start)


def short_transform(grid, left):
    root = math.sqrt(0.5)
    for f in range(2):
        for block in range(3):
            north = [grid[f, 0, :, pl.ds(l * INNER + block * 128, 128)].astype(jnp.float32) for l in range(8)]
            south = [grid[f, 1, :, pl.ds(l * INNER + block * 128, 128)].astype(jnp.float32) for l in range(8)]
            for p in range(2):
                v = [a + b if p == 0 else a - b for a, b in zip(north, south, strict=True)]
                even = [v[l] + v[l + 4] for l in range(4)]
                odd = [v[l] - v[l + 4] for l in range(4)]
                minus = (odd[1] - odd[3]) * root
                plus = (odd[1] + odd[3]) * root
                pieces = (
                    ((even[0] + even[2]) + (even[1] + even[3]), (even[0] + even[2]) - (even[1] + even[3])),
                    (odd[0] + minus, -odd[2] - plus),
                    (even[0] - even[2], even[3] - even[1]),
                    (odd[0] - minus, odd[2] - plus),
                )
                for u in range(4):
                    for part in range(2):
                        left[u, pl.ds(f * 32 + p * 16, 16), pl.ds(part * INNER + block * 128, 128)] = pieces[u][
                            part
                        ].astype(jnp.bfloat16)


def long_transform(left, table, waves):
    for u in range(4):
        product = jnp.dot(left[u], table[u], preferred_element_type=jnp.float32)
        for s in range(2):
            for r in range(2):
                waves[s, pl.ds(r * 64, 64), pl.ds(u * 128, 128)] = product[
                    :, (s * 2 + r) * 128 : (s * 2 + r + 1) * 128
                ].astype(jnp.bfloat16)


def swap_groups(blocks, width):
    lane = lax.broadcasted_iota(jnp.int32, blocks[0].shape, 1)
    blocks = list(blocks)
    bit = 1
    while bit < len(blocks):
        shift = bit * width
        keep = (lane & shift) == 0
        for i in range(len(blocks)):
            if i & bit == 0:
                a, b = blocks[i], blocks[i + bit]
                blocks[i] = jnp.where(keep, a, pltpu.roll(b, shift, 1))
                blocks[i + bit] = jnp.where(keep, pltpu.roll(a, 128 - shift, 1), b)
        bit *= 2
    return blocks


def pick_slots(c, slot_rows, waves, one_hot, picked, outgoing):
    row = lax.broadcasted_iota(jnp.int32, (64, 128), 0) * 8
    for h in range(2):
        slots = jnp.broadcast_to(slot_rows[c, h : h + 1, :], (64, 128))
        for u in range(4):
            for half in range(2):
                here = row + wave_rows(u, half)
                place = (pl.ds(u * 128 + half * 64, 64), pl.ds(h * 128, 128))
                one_hot[(0, *place)] = jnp.where(here == slots, 1.0, 0.0).astype(jnp.bfloat16)
                one_hot[(1, *place)] = jnp.where(here == 511 - slots, 1.0, 0.0).astype(jnp.bfloat16)
    for s in range(2):
        picked[s] = jnp.dot(waves[s], one_hot[s], preferred_element_type=jnp.float32)
    for h in range(2):
        for part in range(2):
            blocks = [
                picked[g // 4, pl.ds((g % 4) * 32 + part * 16, 16), pl.ds(h * 128, 128)] for g in range(8)
            ]
            for k, block in enumerate(swap_groups(blocks, 1)):
                outgoing[h * 8 + k, c, pl.ds(part * 16, 16), :] = block.astype(jnp.bfloat16)


def gather_fields(c, arrived, turned):
    for part in range(2):
        blocks = [arrived[f, c, pl.ds(part * 16, 16), :].astype(jnp.float32) for f in range(FLDS)]
        for i, block in enumerate(swap_groups(blocks, 8)):
            turned[c, i, pl.ds(part * 16, 16), :] = block.astype(jnp.bfloat16)


def kernel(
    grid, slot, seeds, out,
    table, left, waves, one_hot, picked, outgoing, arrived, turned, own_column, all_slots, slot_rows,
    send_list, recv_list, send_lists, recv_lists, send_fld, recv_fld, send_band, recv_band,
):
    band, fld = lax.axis_index("band"), lax.axis_index("fld")
    x, z = band // ZS, band % ZS

    barrier = pltpu.get_barrier_semaphore()

    def greet(axis, me, size):
        def one(d, carry):
            pl.semaphore_signal(barrier, inc=1, device_id={axis: (me + d) % size})
            return carry

        lax.fori_loop(1, size, one, 0)

    greet("fld", fld, FLDS)
    greet("band", band, BANDS)

    make_table(seeds, table)
    short_transform(grid, left)
    own_column[fld] = jnp.full((1, 128), slot[0], jnp.int32)
    pl.semaphore_wait(barrier, FLDS - 1 + BANDS - 1)

    def list_copy(d, source):
        return pltpu.make_async_remote_copy(
            own_column.at[source], own_column.at[source], send_list.at[d], recv_list.at[d],
            device_id={"fld": (fld + d) % FLDS},
        )

    lax.fori_loop(1, FLDS, lambda d, k: (list_copy(d, fld).start(), k)[1], 0)
    long_transform(left, table, waves)
    lax.fori_loop(1, FLDS, lambda d, k: (list_copy(d, (fld + FLDS - d) % FLDS).wait_recv(), k)[1], 0)

    lane = lax.broadcasted_iota(jnp.int32, (1, 128), 1)
    for h in range(2):
        row = jnp.zeros((1, 128), jnp.int32)
        for k in range(8):
            row = row + jnp.where(lane % 8 == k, own_column[h * 8 + k], 0)
        all_slots[band, pl.ds(h, 1), :] = row

    def lists_copy(d, source):
        return pltpu.make_async_remote_copy(
            all_slots.at[source], all_slots.at[source], send_lists.at[d], recv_lists.at[d],
            device_id={"band": (band + d) % BANDS},
        )

    lax.fori_loop(1, BANDS, lambda d, k: (lists_copy(d, band).start(), k)[1], 0)
    lax.fori_loop(1, BANDS, lambda d, k: (lists_copy(d, (band + BANDS - d) % BANDS).wait_recv(), k)[1], 0)
    lanes = lax.broadcasted_iota(jnp.int32, (2, 128), 1)
    for c in range(3):
        rows = jnp.zeros((2, 128), jnp.int32)
        for i in range(16):
            rows = rows + jnp.where(lanes // 8 == i, all_slots[(i // 4) * ZS + (i % 4) * 3 + c], 0)
        slot_rows[c] = rows

    def fld_copy(step, c, d, source):
        return pltpu.make_async_remote_copy(
            outgoing.at[(fld + d) % FLDS, c], arrived.at[source, c], send_fld.at[step, d], recv_fld.at[step, d],
            device_id={"fld": (fld + d) % FLDS},
        )

    def chunk_out(step, carry):
        c = (z + step) % 3
        pick_slots(c, slot_rows, waves, one_hot, picked, outgoing)
        lax.fori_loop(1, FLDS, lambda d, k: (fld_copy(step, c, d, fld).start(), k)[1], 0)
        arrived[fld, c] = outgoing[fld, c]
        return carry

    lax.fori_loop(0, 3, chunk_out, 0)

    def band_copy(step, o, sign):
        dx, dz = o // 4, step + 3 * (o % 4)
        to_x, to_z = (x + dx) % 4, (z + dz) % ZS
        from_x, from_z = (x + 4 - dx) % 4, (z + ZS - dz) % ZS
        source = band if sign else from_x * ZS + from_z
        return pltpu.make_async_remote_copy(
            turned.at[to_z % 3, to_x * 4 + to_z // 3], out.at[source], send_band.at[step, o], recv_band.at[step, o],
            device_id={"band": to_x * ZS + to_z},
        )

    for step in range(3):
        c = (z + step) % 3
        lax.fori_loop(
            1, FLDS, lambda d, k: (fld_copy(step, c, d, (fld + FLDS - d) % FLDS).wait_recv(), k)[1], 0
        )
        gather_fields(c, arrived, turned)
        lax.fori_loop(0 if step else 1, 16, lambda o, k: (band_copy(step, o, True).start(), k)[1], 0)
        if step == 0:
            out[band] = turned[c, x * 4 + z // 3]
    for step in range(3):
        lax.fori_loop(0 if step else 1, 16, lambda o, k: (band_copy(step, o, False).wait_recv(), k)[1], 0)

    lax.fori_loop(1, FLDS, lambda d, k: (list_copy(d, fld).wait_send(), k)[1], 0)
    lax.fori_loop(1, BANDS, lambda d, k: (lists_copy(d, band).wait_send(), k)[1], 0)
    for step in range(3):
        c = (z + step) % 3
        lax.fori_loop(1, FLDS, lambda d, k: (fld_copy(step, c, d, fld).wait_send(), k)[1], 0)
        lax.fori_loop(0 if step else 1, 16, lambda o, k: (band_copy(step, o, True).wait_send(), k)[1], 0)


def folded_at_owner(grid_fields, slot_wave):
    bf16, f32, i32 = jnp.bfloat16, jnp.float32, jnp.int32
    vmem = pl.BlockSpec(memory_space=pltpu.VMEM)
    dma = pltpu.SemaphoreType.DMA
    return pl.pallas_call(
        kernel,
        out_shape=jax.ShapeDtypeStruct((BANDS, 32, 128), bf16),
        in_specs=[vmem, pl.BlockSpec(memory_space=pltpu.SMEM), vmem],
        out_specs=vmem,
        scratch_shapes=[
            pltpu.VMEM((4, 768, 512), bf16),
            pltpu.VMEM((4, 64, 768), bf16),
            pltpu.VMEM((2, 128, 512), bf16),
            pltpu.VMEM((2, 512, 256), bf16),
            pltpu.VMEM((2, 128, 256), f32),
            pltpu.VMEM((FLDS, 3, 32, 128), bf16),
            pltpu.VMEM((FLDS, 3, 32, 128), bf16),
            pltpu.VMEM((3, 16, 32, 128), bf16),
            pltpu.VMEM((FLDS, 1, 128), i32),
            pltpu.VMEM((BANDS, 2, 128), i32),
            pltpu.VMEM((3, 2, 128), i32),
            dma((FLDS,)), dma((FLDS,)), dma((BANDS,)), dma((BANDS,)),
            dma((3, FLDS)), dma((3, FLDS)), dma((3, 16)), dma((3, 16)),
        ],
        compiler_params=pltpu.CompilerParams(collective_id=0, has_side_effects=True),
        name="folded_at_owner",
    )(grid_fields, slot_wave, jnp.asarray(table_seeds()))


def local(grid_fields, legendre, slot_wave):
    folded = folded_at_owner(grid_fields, slot_wave)
    folded = folded.reshape(BANDS, 2, 16, 128)
    table = legendre[0].reshape(2, BANDS, 16, legendre.shape[3])
    products = jnp.einsum("bpjn,pbjc->pnc", folded, table, preferred_element_type=jnp.float32)
    products = products.reshape(2, 16, 2, 2, 2, legendre.shape[3])
    parity = lax.broadcasted_iota(jnp.int32, (2, legendre.shape[3]), 0)
    column = lax.broadcasted_iota(jnp.int32, (2, legendre.shape[3]), 1)
    first_count = (MM - slot_wave[0] + 1 - parity) // 2
    second_count = (slot_wave[0] + 2 - parity) // 2
    first_mask = (column < first_count)[:, None, None, None, :]
    second_mask = ((column >= first_count) & (column < first_count + second_count))[:, None, None, None, :]
    spectrum = jnp.where(first_mask, products[:, :, 0], jnp.where(second_mask, products[:, :, 1], 0.0))
    spectrum = spectrum.astype(jnp.bfloat16).transpose(0, 1, 3, 2, 4)
    return spectrum.reshape(1, 2, 32, 2, legendre.shape[3])


def solution(mesh):
    placed = (P("fld", None, "band", None), P(("band", "fld"), None, None, None), P(("band", "fld")))
    return jax.shard_map(
        local,
        mesh=mesh,
        in_specs=placed,
        out_specs=P(("band", "fld"), None, None, None, None),
        check_vma=False,
    )
```

```python
import math

import jax
import jax.numpy as jnp
import numpy as np
from jax import lax
from jax.experimental import pallas as pl
from jax.experimental.pallas import tpu as pltpu
from jax.sharding import PartitionSpec as P

MM = 1024
NLON = 3072
INNER = 384
BANDS, FLDS = 48, 16
ZS = 12
STEPS = 16


def wave_rows(group, half):
    return group if half == 0 else (4 if group == 0 else 8 - group)


def table_seeds():
    waves = np.zeros((2, 4, 2, 64), np.int64)
    for s in range(2):
        for u in range(4):
            for half in range(2):
                waves[s, u, half] = wave_rows(u, half) + 8 * (64 * s + np.arange(64))
    waves = waves.reshape(1, 1024)
    rows = np.arange(STEPS).reshape(STEPS, 1)
    first = 2.0 * np.pi * ((rows * waves) % NLON) / NLON
    turn = np.broadcast_to(2.0 * np.pi * ((STEPS * waves) % NLON) / NLON, (STEPS, 1024))
    scale = 1.0 / math.sqrt(NLON)
    return np.stack([np.cos(first) * scale, np.sin(first) * scale, np.cos(turn), np.sin(turn)]).astype(np.float32)


def make_table(seeds, table):
    lane = lax.broadcasted_iota(jnp.int32, (STEPS, 128), 1)
    first_half = lane < 64
    for s in range(2):

        def rows(step, carry):
            at = pl.multiple_of(step * STEPS, STEPS)
            after = []
            for u in range(4):
                cosine, sine = carry[u]
                low, high = pl.ds(at, STEPS), pl.ds(at + INNER, STEPS)
                real, imag = pl.ds(s * 256, 128), pl.ds(s * 256 + 128, 128)
                if u == 0:
                    table[u, low, real] = jnp.where(first_half, cosine, 0.0).astype(jnp.bfloat16)
                    table[u, low, imag] = jnp.where(first_half, -sine, 0.0).astype(jnp.bfloat16)
                    table[u, high, real] = jnp.where(first_half, 0.0, cosine).astype(jnp.bfloat16)
                    table[u, high, imag] = jnp.where(first_half, 0.0, -sine).astype(jnp.bfloat16)
                else:
                    table[u, low, real] = cosine.astype(jnp.bfloat16)
                    table[u, low, imag] = (-sine).astype(jnp.bfloat16)
                    table[u, high, real] = jnp.where(first_half, sine, -sine).astype(jnp.bfloat16)
                    table[u, high, imag] = jnp.where(first_half, cosine, -cosine).astype(jnp.bfloat16)
                columns = pl.ds((s * 4 + u) * 128, 128)
                turn_cos, turn_sin = seeds[2, :, columns], seeds[3, :, columns]
                after.append((cosine * turn_cos - sine * turn_sin, sine * turn_cos + cosine * turn_sin))
            return tuple(after)

        start = tuple(
            (seeds[0, :, pl.ds((s * 4 + u) * 128, 128)], seeds[1, :, pl.ds((s * 4 + u) * 128, 128)]) for u in range(4)
        )
        lax.fori_loop(0, INNER // STEPS, rows, start)


def short_transform(grid, left):
    root = math.sqrt(0.5)
    for f in range(2):
        for block in range(3):
            north = [grid[f, 0, :, pl.ds(l * INNER + block * 128, 128)].astype(jnp.float32) for l in range(8)]
            south = [grid[f, 1, :, pl.ds(l * INNER + block * 128, 128)].astype(jnp.float32) for l in range(8)]
            for p in range(2):
                v = [a + b if p == 0 else a - b for a, b in zip(north, south, strict=True)]
                even = [v[l] + v[l + 4] for l in range(4)]
                odd = [v[l] - v[l + 4] for l in range(4)]
                minus = (odd[1] - odd[3]) * root
                plus = (odd[1] + odd[3]) * root
                pieces = (
                    ((even[0] + even[2]) + (even[1] + even[3]), (even[0] + even[2]) - (even[1] + even[3])),
                    (odd[0] + minus, -odd[2] - plus),
                    (even[0] - even[2], even[3] - even[1]),
                    (odd[0] - minus, odd[2] - plus),
                )
                for u in range(4):
                    for part in range(2):
                        left[u, pl.ds(f * 32 + p * 16, 16), pl.ds(part * INNER + block * 128, 128)] = pieces[u][
                            part
                        ].astype(jnp.bfloat16)


def long_transform(left, table, waves):
    for u in range(4):
        product = jnp.dot(left[u], table[u], preferred_element_type=jnp.float32)
        for s in range(2):
            for r in range(2):
                waves[s, pl.ds(r * 64, 64), pl.ds(u * 128, 128)] = product[
                    :, (s * 2 + r) * 128 : (s * 2 + r + 1) * 128
                ].astype(jnp.bfloat16)


def swap_groups(blocks, width):
    lane = lax.broadcasted_iota(jnp.int32, blocks[0].shape, 1)
    blocks = list(blocks)
    bit = 1
    while bit < len(blocks):
        shift = bit * width
        keep = (lane & shift) == 0
        for i in range(len(blocks)):
            if i & bit == 0:
                a, b = blocks[i], blocks[i + bit]
                blocks[i] = jnp.where(keep, a, pltpu.roll(b, shift, 1))
                blocks[i + bit] = jnp.where(keep, pltpu.roll(a, 128 - shift, 1), b)
        bit *= 2
    return blocks


def pick_slots(c, slot_rows, waves, one_hot, picked, outgoing):
    row = lax.broadcasted_iota(jnp.int32, (64, 128), 0) * 8
    for h in range(2):
        slots = jnp.broadcast_to(slot_rows[c, h : h + 1, :], (64, 128))
        for u in range(4):
            for half in range(2):
                here = row + wave_rows(u, half)
                place = (pl.ds(u * 128 + half * 64, 64), pl.ds(h * 128, 128))
                one_hot[(0, *place)] = jnp.where(here == slots, 1.0, 0.0).astype(jnp.bfloat16)
                one_hot[(1, *place)] = jnp.where(here == 511 - slots, 1.0, 0.0).astype(jnp.bfloat16)
    for s in range(2):
        picked[s] = jnp.dot(waves[s], one_hot[s], preferred_element_type=jnp.float32)
    for h in range(2):
        for part in range(2):
            blocks = [
                picked[g // 4, pl.ds((g % 4) * 32 + part * 16, 16), pl.ds(h * 128, 128)] for g in range(8)
            ]
            for k, block in enumerate(swap_groups(blocks, 1)):
                outgoing[h * 8 + k, c, pl.ds(part * 16, 16), :] = block.astype(jnp.bfloat16)


def gather_fields(c, arrived, turned):
    for part in range(2):
        blocks = [arrived[c, f, pl.ds(part * 16, 16), :].astype(jnp.float32) for f in range(FLDS)]
        for i, block in enumerate(swap_groups(blocks, 8)):
            turned[c * 16 + i, pl.ds(part * 16, 16), :] = block.astype(jnp.bfloat16)


def wrap(at, size):
    return jnp.where(at >= size, at - size, at)


def arrived_at(ref, semaphore):
    pltpu.make_async_copy(ref, ref, semaphore).wait()


def each(first, last, act):
    lax.fori_loop(first, last, lambda k, carry: (act(k), carry)[1], 0)


def kernel(
    grid_hbm, slot, seeds_hbm, out,
    grid, seeds, table, left, waves, one_hot, picked, outgoing, arrived, turned, own_column, all_slots, slot_rows, by_row,
    input_sem, send_list, recv_list, send_lists, recv_lists, send_fld, recv_fld, send_band, recv_band,
):
    band, fld = lax.axis_index("band"), lax.axis_index("fld")
    x, z = band // ZS, band % ZS
    inputs = (
        pltpu.make_async_copy(seeds_hbm, seeds, input_sem.at[0]),
        pltpu.make_async_copy(grid_hbm, grid, input_sem.at[1]),
    )

    barrier = pltpu.get_barrier_semaphore()
    each(1, BANDS, lambda d: pl.semaphore_signal(barrier, inc=1, device_id={"band": wrap(band + d, BANDS)}))
    each(1, FLDS, lambda d: pl.semaphore_signal(barrier, inc=1, device_id={"fld": wrap(fld + d, FLDS)}))
    for copy in inputs:
        copy.start()
    own_column[fld] = jnp.full((1, 128), slot[0], jnp.int32)
    pl.semaphore_wait(barrier, FLDS - 1 + BANDS - 1)

    def list_start(d):
        pltpu.make_async_remote_copy(
            own_column.at[fld], own_column.at[fld], send_list, recv_list, device_id={"fld": wrap(fld + d, FLDS)}
        ).start()

    each(1, FLDS, list_start)
    for copy in inputs:
        copy.wait()
    make_table(seeds, table)
    short_transform(grid, left)
    arrived_at(own_column.at[pl.ds(0, FLDS - 1)], recv_list)

    lane = lax.broadcasted_iota(jnp.int32, (1, 128), 1)
    for h in range(2):
        row = jnp.zeros((1, 128), jnp.int32)
        for k in range(8):
            row = row + jnp.where(lane % 8 == k, own_column[h * 8 + k], 0)
        all_slots[band, pl.ds(h, 1), :] = row

    def lists_start(d):
        pltpu.make_async_remote_copy(
            all_slots.at[band], all_slots.at[band], send_lists, recv_lists, device_id={"band": wrap(band + d, BANDS)}
        ).start()

    each(1, BANDS, lists_start)
    long_transform(left, table, waves)
    arrived_at(all_slots.at[pl.ds(0, BANDS - 1)], recv_lists)
    lanes = lax.broadcasted_iota(jnp.int32, (2, 128), 1)
    for c in range(3):
        rows = jnp.zeros((2, 128), jnp.int32)
        for i in range(16):
            rows = rows + jnp.where(lanes // 8 == i, all_slots[(i // 4) * ZS + (i % 4) * 3 + c], 0)
        slot_rows[c] = rows

    def fld_start(step, c, d):
        to = wrap(fld + d, FLDS)
        pltpu.make_async_remote_copy(
            outgoing.at[to, c], arrived.at[c, fld], send_fld, recv_fld.at[step], device_id={"fld": to}
        ).start()

    def chunk_out(step, carry):
        c = (z + step) % 3
        pick_slots(c, slot_rows, waves, one_hot, picked, outgoing)
        each(1, FLDS, lambda d: fld_start(step, c, d))
        arrived[c, fld] = outgoing[fld, c]
        return carry

    lax.fori_loop(0, 3, chunk_out, 0)

    def band_start(step, o):
        to_x, to_z = wrap(x + o // 4, 4), wrap(z + step + 3 * (o % 4), ZS)
        pltpu.make_async_remote_copy(
            turned.at[(to_z % 3) * 16 + to_x * 4 + to_z // 3], by_row.at[band], send_band, recv_band,
            device_id={"band": to_x * ZS + to_z},
        ).start()

    for step in range(3):
        c = (z + step) % 3
        arrived_at(arrived.at[c, pl.ds(0, FLDS - 1)], recv_fld.at[step])
        gather_fields(c, arrived, turned)
        each(0 if step else 1, 16, lambda o: band_start(step, o))
        if step == 0:
            by_row[band] = turned[c * 16 + x * 4 + z // 3]
    arrived_at(own_column.at[pl.ds(0, FLDS - 1)], send_list)
    arrived_at(all_slots.at[pl.ds(0, BANDS - 1)], send_lists)
    arrived_at(outgoing.at[pl.ds(0, FLDS - 1)], send_fld)
    arrived_at(by_row.at[pl.ds(0, BANDS - 1)], recv_band)
    for p in range(2):
        for block in range(6):
            rows = by_row[pl.ds(block * 8, 8), pl.ds(p * 16, 16), :].reshape(128, 128)
            out[p, :, pl.ds(block * 128, 128)] = rows.T
    arrived_at(turned.at[pl.ds(0, BANDS - 1)], send_band)


def folded_at_owner(grid_fields, slot_wave):
    bf16, f32, i32 = jnp.bfloat16, jnp.float32, jnp.int32
    any_space = pl.BlockSpec(memory_space=pl.ANY)
    dma = pltpu.SemaphoreType.DMA
    return pl.pallas_call(
        kernel,
        out_shape=jax.ShapeDtypeStruct((2, 128, BANDS * 16), bf16),
        in_specs=[any_space, pl.BlockSpec(memory_space=pltpu.SMEM), any_space],
        out_specs=pl.BlockSpec(memory_space=pltpu.VMEM),
        scratch_shapes=[
            pltpu.VMEM(grid_fields.shape, bf16),
            pltpu.VMEM((4, STEPS, 1024), f32),
            pltpu.VMEM((4, 768, 512), bf16),
            pltpu.VMEM((4, 64, 768), bf16),
            pltpu.VMEM((2, 128, 512), bf16),
            pltpu.VMEM((2, 512, 256), bf16),
            pltpu.VMEM((2, 128, 256), f32),
            pltpu.VMEM((FLDS, 3, 32, 128), bf16),
            pltpu.VMEM((3, FLDS, 32, 128), bf16),
            pltpu.VMEM((BANDS, 32, 128), bf16),
            pltpu.VMEM((FLDS, 1, 128), i32),
            pltpu.VMEM((BANDS, 2, 128), i32),
            pltpu.VMEM((3, 2, 128), i32),
            pltpu.VMEM((BANDS, 32, 128), bf16),
            dma((2,)), dma, dma, dma, dma, dma, dma((3,)), dma, dma,
        ],
        compiler_params=pltpu.CompilerParams(collective_id=0, has_side_effects=True),
        name="folded_at_owner",
    )(grid_fields, slot_wave, jnp.asarray(table_seeds()))


def local(grid_fields, legendre, slot_wave):
    folded = folded_at_owner(grid_fields, slot_wave)
    products = jnp.einsum("pnj,pjc->pnc", folded, legendre[0], preferred_element_type=jnp.float32)
    products = products.reshape(2, 16, 2, 2, 2, legendre.shape[3])
    parity = lax.broadcasted_iota(jnp.int32, (2, legendre.shape[3]), 0)
    column = lax.broadcasted_iota(jnp.int32, (2, legendre.shape[3]), 1)
    first_count = (MM - slot_wave[0] + 1 - parity) // 2
    second_count = (slot_wave[0] + 2 - parity) // 2
    first_mask = (column < first_count)[:, None, None, None, :]
    second_mask = ((column >= first_count) & (column < first_count + second_count))[:, None, None, None, :]
    spectrum = jnp.where(first_mask, products[:, :, 0], jnp.where(second_mask, products[:, :, 1], 0.0))
    spectrum = spectrum.astype(jnp.bfloat16).transpose(0, 1, 3, 2, 4)
    return spectrum.reshape(1, 2, 32, 2, legendre.shape[3])


def solution(mesh):
    placed = (P("fld", None, "band", None), P(("band", "fld"), None, None, None), P(("band", "fld")))
    return jax.shard_map(
        local,
        mesh=mesh,
        in_specs=placed,
        out_specs=P(("band", "fld"), None, None, None, None),
        check_vma=False,
    )
```

```python
import math

import jax
import jax.numpy as jnp
import numpy as np
from jax import lax
from jax.experimental import pallas as pl
from jax.experimental.pallas import tpu as pltpu
from jax.sharding import PartitionSpec as P

MM = 1024
NLON = 3072
INNER = 384
BANDS, FLDS = 48, 16
ZS = 12
STEPS = 16


def wave_rows(group, half):
    return group if half == 0 else (4 if group == 0 else 8 - group)


def table_seeds():
    waves = np.zeros((2, 4, 2, 64), np.int64)
    for s in range(2):
        for u in range(4):
            for half in range(2):
                waves[s, u, half] = wave_rows(u, half) + 8 * (64 * s + np.arange(64))
    waves = waves.reshape(1, 1024)
    rows = np.arange(STEPS).reshape(STEPS, 1)
    first = 2.0 * np.pi * ((rows * waves) % NLON) / NLON
    turn = np.broadcast_to(2.0 * np.pi * ((STEPS * waves) % NLON) / NLON, (STEPS, 1024))
    scale = 1.0 / math.sqrt(NLON)
    return np.stack([np.cos(first) * scale, np.sin(first) * scale, np.cos(turn), np.sin(turn)]).astype(np.float32)


def make_table(seeds, table):
    lane = lax.broadcasted_iota(jnp.int32, (STEPS, 128), 1)
    first_half = lane < 64
    for s in range(2):

        def rows(step, carry):
            at = pl.multiple_of(step * STEPS, STEPS)
            after = []
            for u in range(4):
                cosine, sine = carry[u]
                low, high = pl.ds(at, STEPS), pl.ds(at + INNER, STEPS)
                real, imag = pl.ds(s * 256, 128), pl.ds(s * 256 + 128, 128)
                if u == 0:
                    table[u, low, real] = jnp.where(first_half, cosine, 0.0).astype(jnp.bfloat16)
                    table[u, low, imag] = jnp.where(first_half, -sine, 0.0).astype(jnp.bfloat16)
                    table[u, high, real] = jnp.where(first_half, 0.0, cosine).astype(jnp.bfloat16)
                    table[u, high, imag] = jnp.where(first_half, 0.0, -sine).astype(jnp.bfloat16)
                else:
                    table[u, low, real] = cosine.astype(jnp.bfloat16)
                    table[u, low, imag] = (-sine).astype(jnp.bfloat16)
                    table[u, high, real] = jnp.where(first_half, sine, -sine).astype(jnp.bfloat16)
                    table[u, high, imag] = jnp.where(first_half, cosine, -cosine).astype(jnp.bfloat16)
                columns = pl.ds((s * 4 + u) * 128, 128)
                turn_cos, turn_sin = seeds[2, :, columns], seeds[3, :, columns]
                after.append((cosine * turn_cos - sine * turn_sin, sine * turn_cos + cosine * turn_sin))
            return tuple(after)

        start = tuple(
            (seeds[0, :, pl.ds((s * 4 + u) * 128, 128)], seeds[1, :, pl.ds((s * 4 + u) * 128, 128)]) for u in range(4)
        )
        lax.fori_loop(0, INNER // STEPS, rows, start)


def short_transform(grid, left):
    root = math.sqrt(0.5)
    for f in range(2):
        for block in range(3):
            north = [grid[f, 0, :, pl.ds(l * INNER + block * 128, 128)].astype(jnp.float32) for l in range(8)]
            south = [grid[f, 1, :, pl.ds(l * INNER + block * 128, 128)].astype(jnp.float32) for l in range(8)]
            for p in range(2):
                v = [a + b if p == 0 else a - b for a, b in zip(north, south, strict=True)]
                even = [v[l] + v[l + 4] for l in range(4)]
                odd = [v[l] - v[l + 4] for l in range(4)]
                minus = (odd[1] - odd[3]) * root
                plus = (odd[1] + odd[3]) * root
                pieces = (
                    ((even[0] + even[2]) + (even[1] + even[3]), (even[0] + even[2]) - (even[1] + even[3])),
                    (odd[0] + minus, -odd[2] - plus),
                    (even[0] - even[2], even[3] - even[1]),
                    (odd[0] - minus, odd[2] - plus),
                )
                for u in range(4):
                    for part in range(2):
                        left[u, pl.ds(f * 32 + p * 16, 16), pl.ds(part * INNER + block * 128, 128)] = pieces[u][
                            part
                        ].astype(jnp.bfloat16)


def long_transform(left, table, waves):
    for u in range(4):
        product = jnp.dot(left[u], table[u], preferred_element_type=jnp.float32)
        for s in range(2):
            for r in range(2):
                waves[s, pl.ds(r * 64, 64), pl.ds(u * 128, 128)] = product[
                    :, (s * 2 + r) * 128 : (s * 2 + r + 1) * 128
                ].astype(jnp.bfloat16)


def swap_groups(blocks, shifts):
    lane = lax.broadcasted_iota(jnp.int32, blocks[0].shape, 1)
    blocks = list(blocks)
    for place, shift in enumerate(shifts):
        bit = 1 << place
        keep = (lane & shift) == 0
        for i in range(len(blocks)):
            if i & bit == 0:
                a, b = blocks[i], blocks[i + bit]
                blocks[i] = jnp.where(keep, a, pltpu.roll(b, shift, 1))
                blocks[i + bit] = jnp.where(keep, pltpu.roll(a, 128 - shift, 1), b)
    return blocks


def pick_slots(c, slot_rows, waves, one_hot, picked, outgoing):
    row = lax.broadcasted_iota(jnp.int32, (64, 128), 0) * 8
    for h in range(2):
        slots = jnp.broadcast_to(slot_rows[c, h : h + 1, :], (64, 128))
        for u in range(4):
            for half in range(2):
                here = row + wave_rows(u, half)
                place = (pl.ds(u * 128 + half * 64, 64), pl.ds(h * 128, 128))
                one_hot[(0, *place)] = jnp.where(here == slots, 1.0, 0.0).astype(jnp.bfloat16)
                one_hot[(1, *place)] = jnp.where(here == 511 - slots, 1.0, 0.0).astype(jnp.bfloat16)
    for s in range(2):
        picked[s] = jnp.dot(waves[s], one_hot[s], preferred_element_type=jnp.float32)
    for h in range(2):
        for part in range(2):
            blocks = [
                picked[g // 4, pl.ds((g % 2) * 64 + (g // 2 % 2) * 32 + part * 16, 16), pl.ds(h * 128, 128)]
                for g in range(8)
            ]
            for k, block in enumerate(swap_groups(blocks, (1, 2, 64))):
                outgoing[h * 8 + k, c, pl.ds(part * 16, 16), :] = block.astype(jnp.bfloat16)


def gather_fields(c, arrived, turned):
    for part in range(2):
        blocks = [arrived[c, f, pl.ds(part * 16, 16), :].astype(jnp.float32) for f in range(FLDS)]
        for i, block in enumerate(swap_groups(blocks, (4, 8, 16, 32))):
            turned[c * 16 + i, pl.ds(part * 16, 16), :] = block.astype(jnp.bfloat16)


def turn_legendre(legendre, by_j):
    first = lax.broadcasted_iota(jnp.int32, (128, 128), 0) == 0
    for block in range(6):
        at = pl.ds(block * 128, 128)
        for c in range(5):
            if c < 4:
                values = legendre[pl.ds(c * 128, 128), :, at].astype(jnp.float32)
            else:
                values = legendre[pl.ds(512, 1), :, at].astype(jnp.float32)
            for p in range(2):
                piece = values[:, p, :]
                if c == 4:
                    piece = jnp.where(first, jnp.broadcast_to(piece, (128, 128)), 0.0)
                by_j[p, at, pl.ds(c * 128, 128)] = piece.astype(jnp.bfloat16).T


def choose_columns(p, wave, products):
    column = lax.broadcasted_iota(jnp.int32, (64, 640), 1)
    first_count = (MM - wave + 1 - p) >> 1
    second_count = (wave + 2 - p) >> 1
    second = jnp.where(column < first_count + second_count, products[64:], 0.0)
    return jnp.where(column < first_count, products[:64], second)


def wrap(at, size):
    return jnp.where(at >= size, at - size, at)


def arrived_at(ref, semaphore):
    pltpu.make_async_copy(ref, ref, semaphore).wait()


def each(first, last, act):
    lax.fori_loop(first, last, lambda k, carry: (act(k), carry)[1], 0)


def kernel(
    grid_hbm, slot_hbm, seeds_hbm, legendre_hbm, out,
    grid, slot, seeds, legendre, by_j, flipped, table, left, waves, one_hot, picked, outgoing, arrived, turned, own_column, all_slots, slot_rows, by_row,
    input_sem, send_list, recv_list, send_lists, recv_lists, send_fld, recv_fld, send_band, recv_band,
):
    band, fld = lax.axis_index("band"), lax.axis_index("fld")
    x, z = band // ZS, band % ZS
    inputs = (
        pltpu.make_async_copy(seeds_hbm, seeds, input_sem.at[0]),
        pltpu.make_async_copy(grid_hbm, grid, input_sem.at[1]),
        pltpu.make_async_copy(legendre_hbm, legendre, input_sem.at[2]),
    )
    own_slot = pltpu.make_async_copy(slot_hbm, slot, input_sem.at[3])
    own_slot.start()

    barrier = pltpu.get_barrier_semaphore()
    each(1, BANDS, lambda d: pl.semaphore_signal(barrier, inc=1, device_id={"band": wrap(band + d, BANDS)}))
    each(1, FLDS, lambda d: pl.semaphore_signal(barrier, inc=1, device_id={"fld": wrap(fld + d, FLDS)}))
    for copy in inputs:
        copy.start()
    own_slot.wait()
    own_column[fld] = jnp.full((1, 128), slot[0], jnp.int32)
    pl.semaphore_wait(barrier, FLDS - 1 + BANDS - 1)

    def list_start(d):
        pltpu.make_async_remote_copy(
            own_column.at[fld], own_column.at[fld], send_list, recv_list, device_id={"fld": wrap(fld + d, FLDS)}
        ).start()

    each(1, FLDS, list_start)
    for copy in inputs[:2]:
        copy.wait()
    make_table(seeds, table)
    short_transform(grid, left)
    arrived_at(own_column.at[pl.ds(0, FLDS - 1)], recv_list)

    lane = lax.broadcasted_iota(jnp.int32, (1, 128), 1)
    for h in range(2):
        row = jnp.zeros((1, 128), jnp.int32)
        for k in range(8):
            row = row + jnp.where(lane // 64 * 4 + lane % 4 == k, own_column[h * 8 + k], 0)
        all_slots[band, pl.ds(h, 1), :] = row

    def lists_start(d):
        pltpu.make_async_remote_copy(
            all_slots.at[band], all_slots.at[band], send_lists, recv_lists, device_id={"band": wrap(band + d, BANDS)}
        ).start()

    each(1, BANDS, lists_start)
    long_transform(left, table, waves)
    arrived_at(all_slots.at[pl.ds(0, BANDS - 1)], recv_lists)
    lanes = lax.broadcasted_iota(jnp.int32, (2, 128), 1)
    for c in range(3):
        rows = jnp.zeros((2, 128), jnp.int32)
        for i in range(16):
            rows = rows + jnp.where(lanes // 4 % 16 == i, all_slots[(i // 4) * ZS + (i % 4) * 3 + c], 0)
        slot_rows[c] = rows

    def fld_start(step, c, d):
        to = wrap(fld + d, FLDS)
        pltpu.make_async_remote_copy(
            outgoing.at[to, c], arrived.at[c, fld], send_fld, recv_fld.at[step], device_id={"fld": to}
        ).start()

    def chunk_out(step, carry):
        c = (z + step) % 3
        pick_slots(c, slot_rows, waves, one_hot, picked, outgoing)
        each(1, FLDS, lambda d: fld_start(step, c, d))
        arrived[c, fld] = outgoing[fld, c]
        return carry

    lax.fori_loop(0, 3, chunk_out, 0)

    def band_start(step, o):
        to_x, to_z = wrap(x + o // 4, 4), wrap(z + step + 3 * (o % 4), ZS)
        pltpu.make_async_remote_copy(
            turned.at[(to_z % 3) * 16 + to_x * 4 + to_z // 3], by_row.at[band], send_band, recv_band,
            device_id={"band": to_x * ZS + to_z},
        ).start()

    for step in range(3):
        c = (z + step) % 3
        arrived_at(arrived.at[c, pl.ds(0, FLDS - 1)], recv_fld.at[step])
        gather_fields(c, arrived, turned)
        each(0 if step else 1, 16, lambda o: band_start(step, o))
        if step == 0:
            by_row[band] = turned[c * 16 + x * 4 + z // 3]
    inputs[2].wait()
    turn_legendre(legendre, by_j)
    arrived_at(own_column.at[pl.ds(0, FLDS - 1)], send_list)
    arrived_at(all_slots.at[pl.ds(0, BANDS - 1)], send_lists)
    arrived_at(outgoing.at[pl.ds(0, FLDS - 1)], send_fld)
    arrived_at(by_row.at[pl.ds(0, BANDS - 1)], recv_band)
    for p in range(2):
        for block in range(6):
            rows = by_row[pl.ds(block * 8, 8), pl.ds(p * 16, 16), :].reshape(128, 128)
            flipped[p, :, pl.ds(block * 128, 128)] = rows.T
    for p in range(2):
        products = jnp.dot(flipped[p], by_j[p], preferred_element_type=jnp.float32)
        out[p] = choose_columns(p, slot[0], products).astype(jnp.bfloat16).reshape(32, 2, 640)[:, :, :513]
    arrived_at(turned.at[pl.ds(0, BANDS - 1)], send_band)


def spectrum_at_owner(grid_fields, slot_wave, legendre):
    bf16, f32, i32 = jnp.bfloat16, jnp.float32, jnp.int32
    hbm = pl.BlockSpec(memory_space=pltpu.HBM)
    dma = pltpu.SemaphoreType.DMA
    operands = grid_fields, slot_wave, jnp.asarray(table_seeds()), legendre
    return pl.pallas_call(
        kernel,
        out_shape=jax.ShapeDtypeStruct((2, 32, 2, legendre.shape[0]), bf16),
        in_specs=[hbm] * 4,
        out_specs=pl.BlockSpec(memory_space=pltpu.VMEM),
        scratch_shapes=[
            pltpu.VMEM(grid_fields.shape, bf16),
            pltpu.SMEM((2,), i32),
            pltpu.VMEM((4, STEPS, 1024), f32),
            pltpu.VMEM(legendre.shape, bf16),
            pltpu.VMEM((2, 768, 640), bf16),
            pltpu.VMEM((2, 128, 768), bf16),
            pltpu.VMEM((4, 768, 512), bf16),
            pltpu.VMEM((4, 64, 768), bf16),
            pltpu.VMEM((2, 128, 512), bf16),
            pltpu.VMEM((2, 512, 256), bf16),
            pltpu.VMEM((2, 128, 256), f32),
            pltpu.VMEM((FLDS, 3, 32, 128), bf16),
            pltpu.VMEM((3, FLDS, 32, 128), bf16),
            pltpu.VMEM((BANDS, 32, 128), bf16),
            pltpu.VMEM((FLDS, 1, 128), i32),
            pltpu.VMEM((BANDS, 2, 128), i32),
            pltpu.VMEM((3, 2, 128), i32),
            pltpu.VMEM((BANDS, 32, 128), bf16),
            dma((4,)), dma, dma, dma, dma, dma, dma((3,)), dma, dma,
        ],
        compiler_params=pltpu.CompilerParams(
            collective_id=0, has_side_effects=True, vmem_limit_bytes=24 * 1024 * 1024
        ),
        name="spectrum_at_owner",
    )(*(pltpu.with_memory_space_constraint(a, pltpu.HBM) for a in operands))


def local(grid_fields, legendre, slot_wave):
    return spectrum_at_owner(grid_fields, slot_wave, legendre[0].transpose(2, 0, 1))[None]


def solution(mesh):
    placed = (P("fld", None, "band", None), P(("band", "fld"), None, None, None), P(("band", "fld")))
    return jax.shard_map(
        local,
        mesh=mesh,
        in_specs=placed,
        out_specs=P(("band", "fld"), None, None, None, None),
        check_vma=False,
    )
```

```python
import math

import jax
import jax.numpy as jnp
import numpy as np
from jax import lax
from jax.experimental import pallas as pl
from jax.experimental.pallas import tpu as pltpu
from jax.sharding import PartitionSpec as P

MM = 1024
NLON = 3072
INNER = 384
BANDS, FLDS = 48, 16
ZS = 12
STEPS = 16


def wave_rows(group, half):
    return group if half == 0 else (4 if group == 0 else 8 - group)


def table_seeds():
    waves = np.zeros((2, 4, 2, 64), np.int64)
    for s in range(2):
        for u in range(4):
            for half in range(2):
                waves[s, u, half] = wave_rows(u, half) + 8 * (64 * s + np.arange(64))
    waves = waves.reshape(1, 1024)
    rows = np.arange(STEPS).reshape(STEPS, 1)
    first = 2.0 * np.pi * ((rows * waves) % NLON) / NLON
    turn = np.broadcast_to(2.0 * np.pi * ((STEPS * waves) % NLON) / NLON, (STEPS, 1024))
    scale = 1.0 / math.sqrt(NLON)
    return np.stack([np.cos(first) * scale, np.sin(first) * scale, np.cos(turn), np.sin(turn)]).astype(np.float32)


def make_table(seeds, table):
    lane = lax.broadcasted_iota(jnp.int32, (STEPS, 128), 1)
    first_half = lane < 64
    for s in range(2):

        def rows(step, carry):
            at = pl.multiple_of(step * STEPS, STEPS)
            after = []
            for u in range(4):
                cosine, sine = carry[u]
                low, high = pl.ds(at, STEPS), pl.ds(at + INNER, STEPS)
                real, imag = pl.ds(s * 256, 128), pl.ds(s * 256 + 128, 128)
                if u == 0:
                    table[u, low, real] = jnp.where(first_half, cosine, 0.0).astype(jnp.bfloat16)
                    table[u, low, imag] = jnp.where(first_half, -sine, 0.0).astype(jnp.bfloat16)
                    table[u, high, real] = jnp.where(first_half, 0.0, cosine).astype(jnp.bfloat16)
                    table[u, high, imag] = jnp.where(first_half, 0.0, -sine).astype(jnp.bfloat16)
                else:
                    table[u, low, real] = cosine.astype(jnp.bfloat16)
                    table[u, low, imag] = (-sine).astype(jnp.bfloat16)
                    table[u, high, real] = jnp.where(first_half, sine, -sine).astype(jnp.bfloat16)
                    table[u, high, imag] = jnp.where(first_half, cosine, -cosine).astype(jnp.bfloat16)
                columns = pl.ds((s * 4 + u) * 128, 128)
                turn_cos, turn_sin = seeds[2, :, columns], seeds[3, :, columns]
                after.append((cosine * turn_cos - sine * turn_sin, sine * turn_cos + cosine * turn_sin))
            return tuple(after)

        start = tuple(
            (seeds[0, :, pl.ds((s * 4 + u) * 128, 128)], seeds[1, :, pl.ds((s * 4 + u) * 128, 128)]) for u in range(4)
        )
        lax.fori_loop(0, INNER // STEPS, rows, start)


def short_transform(grid, left):
    root = math.sqrt(0.5)
    for f in range(2):
        for block in range(3):
            north = [grid[f, 0, :, pl.ds(l * INNER + block * 128, 128)].astype(jnp.float32) for l in range(8)]
            south = [grid[f, 1, :, pl.ds(l * INNER + block * 128, 128)].astype(jnp.float32) for l in range(8)]
            for p in range(2):
                v = [a + b if p == 0 else a - b for a, b in zip(north, south, strict=True)]
                even = [v[l] + v[l + 4] for l in range(4)]
                odd = [v[l] - v[l + 4] for l in range(4)]
                minus = (odd[1] - odd[3]) * root
                plus = (odd[1] + odd[3]) * root
                pieces = (
                    ((even[0] + even[2]) + (even[1] + even[3]), (even[0] + even[2]) - (even[1] + even[3])),
                    (odd[0] + minus, -odd[2] - plus),
                    (even[0] - even[2], even[3] - even[1]),
                    (odd[0] - minus, odd[2] - plus),
                )
                for u in range(4):
                    for part in range(2):
                        left[u, pl.ds(p * 32 + f * 16, 16), pl.ds(part * INNER + block * 128, 128)] = pieces[u][
                            part
                        ].astype(jnp.bfloat16)


def long_transform(left, table, waves):
    for u in range(4):
        product = jnp.dot(left[u], table[u], preferred_element_type=jnp.float32)
        for s in range(2):
            for r in range(2):
                for p in range(2):
                    waves[s, pl.ds(p * 64 + r * 32, 32), pl.ds(u * 128, 128)] = product[
                        p * 32 : p * 32 + 32, (s * 2 + r) * 128 : (s * 2 + r + 1) * 128
                    ].astype(jnp.bfloat16)


def swap_groups(blocks, shifts):
    lane = lax.broadcasted_iota(jnp.int32, blocks[0].shape, 1)
    blocks = list(blocks)
    for place, shift in enumerate(shifts):
        bit = 1 << place
        keep = (lane & shift) == 0
        for i in range(len(blocks)):
            if i & bit == 0:
                a, b = blocks[i], blocks[i + bit]
                blocks[i] = jnp.where(keep, a, pltpu.roll(b, shift, 1))
                blocks[i + bit] = jnp.where(keep, pltpu.roll(a, 128 - shift, 1), b)
    return blocks


def pick_slots(c, p, slot_rows, waves, one_hot, picked, put):
    row = lax.broadcasted_iota(jnp.int32, (64, 128), 0) * 8
    for h in range(2):
        slots = jnp.broadcast_to(slot_rows[p, c, h : h + 1, :], (64, 128))
        for u in range(4):
            for half in range(2):
                here = row + wave_rows(u, half)
                place = (pl.ds(u * 128 + half * 64, 64), pl.ds(h * 128, 128))
                one_hot[(0, *place)] = jnp.where(here == slots, 1.0, 0.0).astype(jnp.bfloat16)
                one_hot[(1, *place)] = jnp.where(here == 511 - slots, 1.0, 0.0).astype(jnp.bfloat16)
    for s in range(2):
        picked[s] = jnp.dot(waves[s, pl.ds(p * 64, 64), :], one_hot[s], preferred_element_type=jnp.float32)
    for h in range(2):
        blocks = [
            picked[g // 4, pl.ds((g % 2) * 32 + (g // 2 % 2) * 16, 16), pl.ds(h * 128, 128)] for g in range(8)
        ]
        for k, block in enumerate(swap_groups(blocks, (1, 2, 64))):
            put(h * 8 + k, block.astype(jnp.bfloat16))


def turn_groups(arrived, c, put):
    blocks = [arrived[c * 16 + f].astype(jnp.float32) for f in range(16)]
    for i, block in enumerate(swap_groups(blocks, (4, 8, 16, 32))):
        put(i, block.astype(jnp.bfloat16))


def turn_legendre(legendre, by_j):
    first = lax.broadcasted_iota(jnp.int32, (128, 128), 0) == 0
    for block in range(6):
        at = pl.ds(block * 128, 128)
        for c in range(5):
            if c < 4:
                values = legendre[pl.ds(c * 128, 128), :, at].astype(jnp.float32)
            else:
                values = legendre[pl.ds(512, 1), :, at].astype(jnp.float32)
            for p in range(2):
                piece = values[:, p, :]
                if c == 4:
                    piece = jnp.where(first, jnp.broadcast_to(piece, (128, 128)), 0.0)
                by_j[p, at, pl.ds(c * 128, 128)] = piece.astype(jnp.bfloat16).T


def choose_columns(p, wave, products):
    column = lax.broadcasted_iota(jnp.int32, (64, 640), 1)
    first_count = (MM - wave + 1 - p) >> 1
    second_count = (wave + 2 - p) >> 1
    second = jnp.where(column < first_count + second_count, products[64:], 0.0)
    return jnp.where(column < first_count, products[:64], second)


def wrap(at, size):
    return jnp.where(at >= size, at - size, at)


def arrived_at(ref, semaphore):
    pltpu.make_async_copy(ref, ref, semaphore).wait()


def each(first, last, act):
    lax.fori_loop(first, last, lambda k, carry: (act(k), carry)[1], 0)


def kernel(
    grid_hbm, slot_hbm, seeds_hbm, legendre_hbm, out,
    grid, slot, seeds, legendre, by_j, flipped, table, left, waves, one_hot, picked,
    own_column, all_slots, slot_rows, by_fld, from_fld, by_band, from_band, by_fld_late, from_fld_late, by_band_late, rows,
    input_sem, send_list, recv_list, send_lists, recv_lists,
    send_fld, recv_fld, send_band, recv_band, send_fld_late, recv_fld_late, send_band_late, recv_band_late,
):
    band, fld = lax.axis_index("band"), lax.axis_index("fld")
    x, z = band // ZS, band % ZS
    place = z % 3 * 16 + x * 4 + z // 3
    inputs = (
        pltpu.make_async_copy(seeds_hbm, seeds, input_sem.at[0]),
        pltpu.make_async_copy(grid_hbm, grid, input_sem.at[1]),
        pltpu.make_async_copy(legendre_hbm, legendre, input_sem.at[2]),
    )
    own_slot = pltpu.make_async_copy(slot_hbm, slot, input_sem.at[3])
    own_slot.start()

    barrier = pltpu.get_barrier_semaphore()
    each(1, BANDS, lambda d: pl.semaphore_signal(barrier, inc=1, device_id={"band": wrap(band + d, BANDS)}))
    each(1, FLDS, lambda d: pl.semaphore_signal(barrier, inc=1, device_id={"fld": wrap(fld + d, FLDS)}))
    for copy in inputs:
        copy.start()
    own_slot.wait()
    own_column[fld] = jnp.full((1, 128), slot[0], jnp.int32)
    pl.semaphore_wait(barrier, FLDS - 1 + BANDS - 1)

    def list_start(d):
        pltpu.make_async_remote_copy(
            own_column.at[fld], own_column.at[fld], send_list, recv_list, device_id={"fld": wrap(fld + d, FLDS)}
        ).start()

    each(1, FLDS, list_start)
    for copy in inputs[:2]:
        copy.wait()
    make_table(seeds, table)
    short_transform(grid, left)
    arrived_at(own_column.at[pl.ds(0, FLDS - 1)], recv_list)

    lane = lax.broadcasted_iota(jnp.int32, (1, 128), 1)
    of_eight, of_sixteen = lane // 64 * 4 + lane % 4, lane // 4 % 16
    column = [own_column[f] for f in range(FLDS)]
    for h in range(2):
        row = jnp.zeros((1, 128), jnp.int32)
        for k in range(8):
            row = row + jnp.where(of_eight == k, column[h * 8 + k], 0)
        all_slots[band, pl.ds(h, 1), :] = row
    row = jnp.zeros((1, 128), jnp.int32)
    for f in range(FLDS):
        row = row + jnp.where(of_sixteen == f, column[f], 0)
    all_slots[band, pl.ds(2, 1), :] = row
    all_slots[band, pl.ds(3, 1), :] = jnp.zeros((1, 128), jnp.int32)

    def lists_start(d):
        pltpu.make_async_remote_copy(
            all_slots.at[band], all_slots.at[band], send_lists, recv_lists, device_id={"band": wrap(band + d, BANDS)}
        ).start()

    each(1, BANDS, lists_start)
    long_transform(left, table, waves)
    inputs[2].wait()
    turn_legendre(legendre, by_j)
    arrived_at(all_slots.at[pl.ds(0, BANDS - 1)], recv_lists)
    for c in range(3):
        members = [(i // 4) * ZS + (i % 4) * 3 + c for i in range(16)]
        early = jnp.zeros((2, 128), jnp.int32)
        for i in range(16):
            early = early + jnp.where(of_sixteen == i, all_slots[members[i], pl.ds(0, 2), :], 0)
        slot_rows[0, c] = early
        for h in range(2):
            late = jnp.zeros((1, 128), jnp.int32)
            for k in range(8):
                late = late + jnp.where(of_eight == k, all_slots[members[h * 8 + k], pl.ds(2, 1), :], 0)
            slot_rows[1, c, pl.ds(h, 1), :] = late

    def to_fld(source, target, send, recv, step, c, d):
        to = wrap(fld + d, FLDS)
        pltpu.make_async_remote_copy(
            source.at[to, c], target.at[c * 16 + fld], send, recv.at[step], device_id={"fld": to}
        ).start()

    def to_band(step, o):
        to_x, to_z = wrap(x + o // 4, 4), wrap(z + step + 3 * (o % 4), ZS)
        return to_z % 3 * 16 + to_x * 4 + to_z // 3, {"band": to_x * ZS + to_z}

    def band_start(step, o):
        i, to = to_band(step, o)
        pltpu.make_async_remote_copy(
            by_band.at[i], from_band.at[place], send_band, recv_band.at[step], device_id=to
        ).start()

    def band_late_start(step, o):
        i, to = to_band(step, o)
        pltpu.make_async_remote_copy(
            by_band_late.at[i], rows.at[0, band], send_band_late, recv_band_late, device_id=to
        ).start()

    def chunk_out(step, carry):
        c = (z + step) % 3

        def put_band(i, block):
            by_band[c * 16 + i] = block

        def put_fld(f, block):
            by_fld[f, c] = block

        pick_slots(c, 1, slot_rows, waves, one_hot, picked, put_band)
        each(jnp.where(step == 0, 1, 0), 16, lambda o: band_start(step, o))
        pick_slots(c, 0, slot_rows, waves, one_hot, picked, put_fld)
        each(1, FLDS, lambda d: to_fld(by_fld, from_fld, send_fld, recv_fld, step, c, d))
        from_fld[c * 16 + fld] = by_fld[fld, c]
        return carry

    lax.fori_loop(0, 3, chunk_out, 0)
    from_band[place] = by_band[place]

    for step in range(3):
        c = (z + step) % 3

        def put_band_late(i, block, c=c):
            by_band_late[c * 16 + i] = block

        arrived_at(from_fld.at[pl.ds(c * 16, FLDS - 1)], recv_fld.at[step])
        turn_groups(from_fld, c, put_band_late)
        each(0 if step else 1, 16, lambda o, step=step: band_late_start(step, o))
    rows[0, band] = by_band_late[place]

    for step in range(3):
        c = (z + 3 - step) % 3

        def put_fld_late(f, block, c=c):
            by_fld_late[f, c] = block

        arrived_at(from_band.at[pl.ds(c * 16, 16 if step else 15)], recv_band.at[step])
        turn_groups(from_band, c, put_fld_late)
        each(1, FLDS, lambda d, step=step, c=c: to_fld(by_fld_late, from_fld_late, send_fld_late, recv_fld_late, step, c, d))
        from_fld_late[c * 16 + fld] = by_fld_late[fld, c]

    def finish(p):
        for block in range(6):
            piece = rows[p, pl.ds(block * 8, 8)].reshape(128, 128)
            flipped[p, :, pl.ds(block * 128, 128)] = piece.T
        products = jnp.dot(flipped[p], by_j[p], preferred_element_type=jnp.float32)
        out[p] = choose_columns(p, slot[0], products).astype(jnp.bfloat16).reshape(32, 2, 640)[:, :, :513]

    arrived_at(own_column.at[pl.ds(0, FLDS - 1)], send_list)
    arrived_at(all_slots.at[pl.ds(0, BANDS - 1)], send_lists)
    arrived_at(by_fld.at[pl.ds(0, FLDS - 1)], send_fld)
    arrived_at(by_band.at[pl.ds(0, BANDS - 1)], send_band)
    for step in range(3):
        c = (z + 3 - step) % 3

        def put_row(i, block, c=c):
            rows[1, (i // 4) * ZS + (i % 4) * 3 + c] = block

        arrived_at(from_fld_late.at[pl.ds(c * 16, FLDS - 1)], recv_fld_late.at[step])
        turn_groups(from_fld_late, c, put_row)
    finish(1)
    arrived_at(rows.at[0, pl.ds(0, BANDS - 1)], recv_band_late)
    finish(0)
    arrived_at(by_fld_late.at[pl.ds(0, FLDS - 1)], send_fld_late)
    arrived_at(by_band_late.at[pl.ds(0, BANDS - 1)], send_band_late)


def spectrum_at_owner(grid_fields, slot_wave, legendre):
    bf16, f32, i32 = jnp.bfloat16, jnp.float32, jnp.int32
    hbm = pl.BlockSpec(memory_space=pltpu.HBM)
    dma = pltpu.SemaphoreType.DMA
    operands = grid_fields, slot_wave, jnp.asarray(table_seeds()), legendre
    return pl.pallas_call(
        kernel,
        out_shape=jax.ShapeDtypeStruct((2, 32, 2, legendre.shape[0]), bf16),
        in_specs=[hbm] * 4,
        out_specs=pl.BlockSpec(memory_space=pltpu.VMEM),
        scratch_shapes=[
            pltpu.VMEM(grid_fields.shape, bf16),
            pltpu.SMEM((2,), i32),
            pltpu.VMEM((4, STEPS, 1024), f32),
            pltpu.VMEM(legendre.shape, bf16),
            pltpu.VMEM((2, 768, 640), bf16),
            pltpu.VMEM((2, 128, 768), bf16),
            pltpu.VMEM((4, 768, 512), bf16),
            pltpu.VMEM((4, 64, 768), bf16),
            pltpu.VMEM((2, 128, 512), bf16),
            pltpu.VMEM((2, 512, 256), bf16),
            pltpu.VMEM((2, 64, 256), f32),
            pltpu.VMEM((FLDS, 1, 128), i32),
            pltpu.VMEM((BANDS, 4, 128), i32),
            pltpu.VMEM((2, 3, 2, 128), i32),
            pltpu.VMEM((FLDS, 3, 16, 128), bf16),
            pltpu.VMEM((48, 16, 128), bf16),
            pltpu.VMEM((48, 16, 128), bf16),
            pltpu.VMEM((48, 16, 128), bf16),
            pltpu.VMEM((FLDS, 3, 16, 128), bf16),
            pltpu.VMEM((48, 16, 128), bf16),
            pltpu.VMEM((48, 16, 128), bf16),
            pltpu.VMEM((2, BANDS, 16, 128), bf16),
            dma((4,)), dma, dma, dma, dma,
            dma, dma((3,)), dma, dma((3,)), dma, dma((3,)), dma, dma,
        ],
        compiler_params=pltpu.CompilerParams(
            collective_id=0, has_side_effects=True, vmem_limit_bytes=24 * 1024 * 1024
        ),
        name="spectrum_at_owner",
    )(*(pltpu.with_memory_space_constraint(a, pltpu.HBM) for a in operands))


def local(grid_fields, legendre, slot_wave):
    return spectrum_at_owner(grid_fields, slot_wave, legendre[0].transpose(2, 0, 1))[None]


def solution(mesh):
    placed = (P("fld", None, "band", None), P(("band", "fld"), None, None, None), P(("band", "fld")))
    return jax.shard_map(
        local,
        mesh=mesh,
        in_specs=placed,
        out_specs=P(("band", "fld"), None, None, None, None),
        check_vma=False,
    )
```

```python
import functools
import math

import jax
import jax.numpy as jnp
import numpy as np
from jax import lax
from jax.experimental import pallas as pl
from jax.experimental.pallas import tpu as pltpu
from jax.sharding import PartitionSpec as P

MM = 1024
NLON = 3072
INNER = 384
BANDS, FLDS = 48, 16
ZS = 12
STEPS = 16


def wave_rows(group, half):
    return group if half == 0 else (4 if group == 0 else 8 - group)


def table_seeds():
    waves = np.zeros((2, 4, 2, 64), np.int64)
    for s in range(2):
        for u in range(4):
            for half in range(2):
                waves[s, u, half] = wave_rows(u, half) + 8 * (64 * s + np.arange(64))
    waves = waves.reshape(1, 1024)
    rows = np.arange(STEPS).reshape(STEPS, 1)
    first = 2.0 * np.pi * ((rows * waves) % NLON) / NLON
    turn = np.broadcast_to(2.0 * np.pi * ((STEPS * waves) % NLON) / NLON, (STEPS, 1024))
    scale = 1.0 / math.sqrt(NLON)
    return np.stack([np.cos(first) * scale, np.sin(first) * scale, np.cos(turn), np.sin(turn)]).astype(np.float32)


def make_table(seeds, table):
    lane = lax.broadcasted_iota(jnp.int32, (STEPS, 128), 1)
    first_half = lane < 64
    for s in range(2):

        def rows(step, carry):
            at = pl.multiple_of(step * STEPS, STEPS)
            after = []
            for u in range(4):
                cosine, sine = carry[u]
                low, high = pl.ds(at, STEPS), pl.ds(at + INNER, STEPS)
                real, imag = pl.ds(s * 256, 128), pl.ds(s * 256 + 128, 128)
                if u == 0:
                    table[u, low, real] = jnp.where(first_half, cosine, 0.0).astype(jnp.bfloat16)
                    table[u, low, imag] = jnp.where(first_half, -sine, 0.0).astype(jnp.bfloat16)
                    table[u, high, real] = jnp.where(first_half, 0.0, cosine).astype(jnp.bfloat16)
                    table[u, high, imag] = jnp.where(first_half, 0.0, -sine).astype(jnp.bfloat16)
                else:
                    table[u, low, real] = cosine.astype(jnp.bfloat16)
                    table[u, low, imag] = (-sine).astype(jnp.bfloat16)
                    table[u, high, real] = jnp.where(first_half, sine, -sine).astype(jnp.bfloat16)
                    table[u, high, imag] = jnp.where(first_half, cosine, -cosine).astype(jnp.bfloat16)
                columns = pl.ds((s * 4 + u) * 128, 128)
                turn_cos, turn_sin = seeds[2, :, columns], seeds[3, :, columns]
                after.append((cosine * turn_cos - sine * turn_sin, sine * turn_cos + cosine * turn_sin))
            return tuple(after)

        start = tuple(
            (seeds[0, :, pl.ds((s * 4 + u) * 128, 128)], seeds[1, :, pl.ds((s * 4 + u) * 128, 128)]) for u in range(4)
        )
        lax.fori_loop(0, INNER // STEPS, rows, start)


def short_transform(grid, left):
    root = math.sqrt(0.5)
    for f in range(2):
        for block in range(3):
            north = [grid[f, 0, :, pl.ds(l * INNER + block * 128, 128)].astype(jnp.float32) for l in range(8)]
            south = [grid[f, 1, :, pl.ds(l * INNER + block * 128, 128)].astype(jnp.float32) for l in range(8)]
            for p in range(2):
                v = [a + b if p == 0 else a - b for a, b in zip(north, south, strict=True)]
                even = [v[l] + v[l + 4] for l in range(4)]
                odd = [v[l] - v[l + 4] for l in range(4)]
                minus = (odd[1] - odd[3]) * root
                plus = (odd[1] + odd[3]) * root
                pieces = (
                    ((even[0] + even[2]) + (even[1] + even[3]), (even[0] + even[2]) - (even[1] + even[3])),
                    (odd[0] + minus, -odd[2] - plus),
                    (even[0] - even[2], even[3] - even[1]),
                    (odd[0] - minus, odd[2] - plus),
                )
                for u in range(4):
                    for part in range(2):
                        left[u, pl.ds(p * 32 + f * 16, 16), pl.ds(part * INNER + block * 128, 128)] = pieces[u][
                            part
                        ].astype(jnp.bfloat16)


def long_transform(left, table, waves):
    for u in range(4):
        product = jnp.dot(left[u], table[u], preferred_element_type=jnp.float32)
        for s in range(2):
            for r in range(2):
                for p in range(2):
                    waves[s, pl.ds(p * 64 + r * 32, 32), pl.ds(u * 128, 128)] = product[
                        p * 32 : p * 32 + 32, (s * 2 + r) * 128 : (s * 2 + r + 1) * 128
                    ].astype(jnp.bfloat16)


def swap_groups(blocks, shifts):
    lane = lax.broadcasted_iota(jnp.int32, blocks[0].shape, 1)
    blocks = list(blocks)
    for place, shift in enumerate(shifts):
        bit = 1 << place
        keep = (lane & shift) == 0
        for i in range(len(blocks)):
            if i & bit == 0:
                a, b = blocks[i], blocks[i + bit]
                blocks[i] = jnp.where(keep, a, pltpu.roll(b, shift, 1))
                blocks[i + bit] = jnp.where(keep, pltpu.roll(a, 128 - shift, 1), b)
    return blocks


def pick_slots(c, slot_rows, waves, one_hot, picked, puts):
    row = lax.broadcasted_iota(jnp.int32, (64, 128), 0) * 8
    for p in (1, 0):
        for h in range(2):
            slots = jnp.broadcast_to(slot_rows[p, c, h : h + 1, :], (64, 128))
            for u in range(4):
                for half in range(2):
                    here = row + wave_rows(u, half)
                    place = (pl.ds(u * 128 + half * 64, 64), pl.ds(h * 128, 128))
                    one_hot[(p, 0, *place)] = jnp.where(here == slots, 1.0, 0.0).astype(jnp.bfloat16)
                    one_hot[(p, 1, *place)] = jnp.where(here == 511 - slots, 1.0, 0.0).astype(jnp.bfloat16)
        for s in range(2):
            picked[p, s] = jnp.dot(
                waves[s, pl.ds(p * 64, 64), :], one_hot[p, s], preferred_element_type=jnp.float32
            )
    for p in (1, 0):
        for h in range(2):
            blocks = [
                picked[p, g // 4, pl.ds((g % 2) * 32 + (g // 2 % 2) * 16, 16), pl.ds(h * 128, 128)] for g in range(8)
            ]
            for k, block in enumerate(swap_groups(blocks, (1, 2, 64))):
                puts[p](h * 8 + k, block.astype(jnp.bfloat16))


def turn_groups(arrived, c, put):
    blocks = [arrived[c * 16 + f].astype(jnp.float32) for f in range(16)]
    for i, block in enumerate(swap_groups(blocks, (4, 8, 16, 32))):
        put(i, block.astype(jnp.bfloat16))


def turn_legendre(legendre, by_j):
    first = lax.broadcasted_iota(jnp.int32, (128, 128), 0) == 0
    for block in range(6):
        at = pl.ds(block * 128, 128)
        for c in range(5):
            if c < 4:
                values = legendre[pl.ds(c * 128, 128), :, at].astype(jnp.float32)
            else:
                values = legendre[pl.ds(512, 1), :, at].astype(jnp.float32)
            for p in range(2):
                piece = values[:, p, :]
                if c == 4:
                    piece = jnp.where(first, jnp.broadcast_to(piece, (128, 128)), 0.0)
                by_j[p, at, pl.ds(c * 128, 128)] = piece.astype(jnp.bfloat16).T


def choose_columns(p, wave, products):
    column = lax.broadcasted_iota(jnp.int32, (64, 640), 1)
    first_count = (MM - wave + 1 - p) >> 1
    second_count = (wave + 2 - p) >> 1
    second = jnp.where(column < first_count + second_count, products[64:], 0.0)
    return jnp.where(column < first_count, products[:64], second)


def wrap(at, size):
    return jnp.where(at >= size, at - size, at)


def arrived_at(ref, semaphore):
    pltpu.make_async_copy(ref, ref, semaphore).wait()


def kernel(
    grid_hbm, slot_hbm, seeds_hbm, legendre_hbm, out,
    grid, slot, seeds, legendre, by_j, flipped, table, left, waves, one_hot, picked,
    own_column, all_slots, slot_rows, by_fld, from_fld, by_band, from_band, by_fld_late, from_fld_late, by_band_late, rows,
    input_sem, send_list, recv_list, send_lists, recv_lists,
    send_fld, recv_fld, send_band, recv_band, send_fld_late, recv_fld_late, send_band_late, recv_band_late,
):
    band, fld = lax.axis_index("band"), lax.axis_index("fld")
    x, z = band // ZS, band % ZS
    place = z % 3 * 16 + x * 4 + z // 3
    inputs = (
        pltpu.make_async_copy(seeds_hbm, seeds, input_sem.at[0]),
        pltpu.make_async_copy(grid_hbm, grid, input_sem.at[1]),
        pltpu.make_async_copy(legendre_hbm, legendre, input_sem.at[2]),
    )
    own_slot = pltpu.make_async_copy(slot_hbm, slot, input_sem.at[3])
    own_slot.start()

    all_x = [wrap(x + dx, 4) for dx in range(4)]
    all_z = [wrap(z + dz, ZS) for dz in range(ZS)]
    hops = sorted(((min(dx, 4 - dx) + min(dz, ZS - dz), dx, dz) for dx in range(4) for dz in range(ZS)), reverse=True)
    band_peers = [{"band": all_x[dx] * ZS + all_z[dz]} for far, dx, dz in hops if far]
    fld_peers = [{"fld": wrap(fld + d, FLDS)} for d in sorted(range(1, FLDS), key=lambda d: -min(d, FLDS - d))]

    barrier = pltpu.get_barrier_semaphore()
    for to in band_peers:
        pl.semaphore_signal(barrier, inc=1, device_id=to)
    for to in fld_peers:
        pl.semaphore_signal(barrier, inc=1, device_id=to)
    for copy in inputs:
        copy.start()
    own_slot.wait()
    own_column[fld] = jnp.full((1, 128), slot[0], jnp.int32)
    pl.semaphore_wait(barrier, FLDS - 1 + BANDS - 1)

    for to in fld_peers:
        pltpu.make_async_remote_copy(
            own_column.at[fld], own_column.at[fld], send_list, recv_list, device_id=to
        ).start()
    for copy in inputs[:2]:
        copy.wait()
    make_table(seeds, table)
    short_transform(grid, left)
    arrived_at(own_column.at[pl.ds(0, FLDS - 1)], recv_list)

    lane = lax.broadcasted_iota(jnp.int32, (1, 128), 1)
    of_eight, of_sixteen = lane // 64 * 4 + lane % 4, lane // 4 % 16
    column = [own_column[f] for f in range(FLDS)]
    for h in range(2):
        row = jnp.zeros((1, 128), jnp.int32)
        for k in range(8):
            row = row + jnp.where(of_eight == k, column[h * 8 + k], 0)
        all_slots[band, pl.ds(h, 1), :] = row
    row = jnp.zeros((1, 128), jnp.int32)
    for f in range(FLDS):
        row = row + jnp.where(of_sixteen == f, column[f], 0)
    all_slots[band, pl.ds(2, 1), :] = row
    all_slots[band, pl.ds(3, 1), :] = jnp.zeros((1, 128), jnp.int32)

    for to in band_peers:
        pltpu.make_async_remote_copy(
            all_slots.at[band], all_slots.at[band], send_lists, recv_lists, device_id=to
        ).start()
    long_transform(left, table, waves)
    inputs[2].wait()
    turn_legendre(legendre, by_j)
    arrived_at(all_slots.at[pl.ds(0, BANDS - 1)], recv_lists)
    for c in range(3):
        members = [(i // 4) * ZS + (i % 4) * 3 + c for i in range(16)]
        early = jnp.zeros((2, 128), jnp.int32)
        for i in range(16):
            early = early + jnp.where(of_sixteen == i, all_slots[members[i], pl.ds(0, 2), :], 0)
        slot_rows[0, c] = early
        for h in range(2):
            late = jnp.zeros((1, 128), jnp.int32)
            for k in range(8):
                late = late + jnp.where(of_eight == k, all_slots[members[h * 8 + k], pl.ds(2, 1), :], 0)
            slot_rows[1, c, pl.ds(h, 1), :] = late

    def to_fld(source, target, send, recv, step, c):
        for to in fld_peers:
            pltpu.make_async_remote_copy(
                source.at[to["fld"], c], target.at[c * 16 + fld], send, recv.at[step], device_id=to
            ).start()

    def to_band(step, send):
        c = wrap(z % 3 + step, 3)
        to_z = [wrap(z + step + 3 * k, ZS) for k in range(4)]
        high = [(at - c) // 3 for at in to_z]
        for k in range(4):
            for dx in range(4):
                act = functools.partial(
                    send, c * 16 + all_x[dx] * 4 + high[k], {"band": all_x[dx] * ZS + to_z[k]}
                )
                if k == dx == 0:
                    if isinstance(step, int):
                        if step:
                            act()
                    else:
                        pl.when(step > 0)(act)
                else:
                    act()

    def chunk_out(step, carry):
        c = (z + step) % 3

        def put_band(i, block):
            by_band[c * 16 + i] = block

        def put_fld(f, block):
            by_fld[f, c] = block

        pick_slots(c, slot_rows, waves, one_hot, picked, (put_fld, put_band))
        to_band(step, lambda i, to: pltpu.make_async_remote_copy(
            by_band.at[i], from_band.at[place], send_band, recv_band.at[step], device_id=to
        ).start())
        to_fld(by_fld, from_fld, send_fld, recv_fld, step, c)
        from_fld[c * 16 + fld] = by_fld[fld, c]
        return carry

    lax.fori_loop(0, 3, chunk_out, 0)
    from_band[place] = by_band[place]

    def middle_fld(step):
        c = (z + step) % 3

        def put_band_late(i, block):
            by_band_late[c * 16 + i] = block

        arrived_at(from_fld.at[pl.ds(c * 16, FLDS - 1)], recv_fld.at[step])
        turn_groups(from_fld, c, put_band_late)
        to_band(step, lambda i, to: pltpu.make_async_remote_copy(
            by_band_late.at[i], rows.at[0, band], send_band_late, recv_band_late, device_id=to
        ).start())
        if step == 0:
            rows[0, band] = by_band_late[place]

    def middle_band(step):
        c = (z + 3 - step) % 3

        def put_fld_late(f, block):
            by_fld_late[f, c] = block

        arrived_at(from_band.at[pl.ds(c * 16, 16 if step else 15)], recv_band.at[step])
        turn_groups(from_band, c, put_fld_late)
        to_fld(by_fld_late, from_fld_late, send_fld_late, recv_fld_late, step, c)
        from_fld_late[c * 16 + fld] = by_fld_late[fld, c]

    middle_fld(0)
    middle_fld(1)
    middle_band(0)
    middle_fld(2)
    middle_band(1)
    middle_band(2)

    def finish(p):
        for block in range(6):
            piece = rows[p, pl.ds(block * 8, 8)].reshape(128, 128)
            flipped[p, :, pl.ds(block * 128, 128)] = piece.T
        products = jnp.dot(flipped[p], by_j[p], preferred_element_type=jnp.float32)
        out[p] = choose_columns(p, slot[0], products).astype(jnp.bfloat16).reshape(32, 2, 640)[:, :, :513]

    arrived_at(own_column.at[pl.ds(0, FLDS - 1)], send_list)
    arrived_at(all_slots.at[pl.ds(0, BANDS - 1)], send_lists)
    arrived_at(by_fld.at[pl.ds(0, FLDS - 1)], send_fld)
    arrived_at(by_band.at[pl.ds(0, BANDS - 1)], send_band)
    def last_fld(step):
        c = (z + 3 - step) % 3

        def put_row(i, block):
            rows[1, (i // 4) * ZS + (i % 4) * 3 + c] = block

        arrived_at(from_fld_late.at[pl.ds(c * 16, FLDS - 1)], recv_fld_late.at[step])
        turn_groups(from_fld_late, c, put_row)

    last_fld(0)
    last_fld(1)
    arrived_at(rows.at[0, pl.ds(0, BANDS - 1)], recv_band_late)
    finish(0)
    last_fld(2)
    finish(1)
    arrived_at(by_fld_late.at[pl.ds(0, FLDS - 1)], send_fld_late)
    arrived_at(by_band_late.at[pl.ds(0, BANDS - 1)], send_band_late)


def spectrum_at_owner(grid_fields, slot_wave, legendre):
    bf16, f32, i32 = jnp.bfloat16, jnp.float32, jnp.int32
    hbm = pl.BlockSpec(memory_space=pltpu.HBM)
    dma = pltpu.SemaphoreType.DMA
    operands = grid_fields, slot_wave, jnp.asarray(table_seeds()), legendre
    return pl.pallas_call(
        kernel,
        out_shape=jax.ShapeDtypeStruct((2, 32, 2, legendre.shape[0]), bf16),
        in_specs=[hbm] * 4,
        out_specs=pl.BlockSpec(memory_space=pltpu.VMEM),
        scratch_shapes=[
            pltpu.VMEM(grid_fields.shape, bf16),
            pltpu.SMEM((2,), i32),
            pltpu.VMEM((4, STEPS, 1024), f32),
            pltpu.VMEM(legendre.shape, bf16),
            pltpu.VMEM((2, 768, 640), bf16),
            pltpu.VMEM((2, 128, 768), bf16),
            pltpu.VMEM((4, 768, 512), bf16),
            pltpu.VMEM((4, 64, 768), bf16),
            pltpu.VMEM((2, 128, 512), bf16),
            pltpu.VMEM((2, 2, 512, 256), bf16),
            pltpu.VMEM((2, 2, 64, 256), f32),
            pltpu.VMEM((FLDS, 1, 128), i32),
            pltpu.VMEM((BANDS, 4, 128), i32),
            pltpu.VMEM((2, 3, 2, 128), i32),
            pltpu.VMEM((FLDS, 3, 16, 128), bf16),
            pltpu.VMEM((48, 16, 128), bf16),
            pltpu.VMEM((48, 16, 128), bf16),
            pltpu.VMEM((48, 16, 128), bf16),
            pltpu.VMEM((FLDS, 3, 16, 128), bf16),
            pltpu.VMEM((48, 16, 128), bf16),
            pltpu.VMEM((48, 16, 128), bf16),
            pltpu.VMEM((2, BANDS, 16, 128), bf16),
            dma((4,)), dma, dma, dma, dma,
            dma, dma((3,)), dma, dma((3,)), dma, dma((3,)), dma, dma,
        ],
        compiler_params=pltpu.CompilerParams(
            collective_id=0, has_side_effects=True, vmem_limit_bytes=24 * 1024 * 1024
        ),
        name="spectrum_at_owner",
    )(*(pltpu.with_memory_space_constraint(a, pltpu.HBM) for a in operands))


def local(grid_fields, legendre, slot_wave):
    return spectrum_at_owner(grid_fields, slot_wave, legendre[0].transpose(2, 0, 1))[None]


def solution(mesh):
    placed = (P("fld", None, "band", None), P(("band", "fld"), None, None, None), P(("band", "fld")))
    return jax.shard_map(
        local,
        mesh=mesh,
        in_specs=placed,
        out_specs=P(("band", "fld"), None, None, None, None),
        check_vma=False,
    )
```

```python
import functools
import math

import jax
import jax.numpy as jnp
import numpy as np
from jax import lax
from jax.experimental import pallas as pl
from jax.experimental.pallas import tpu as pltpu
from jax.sharding import PartitionSpec as P

MM = 1024
NLON = 3072
INNER = 384
BANDS, FLDS = 48, 16
ZS = 12
STEPS = 16


def wave_rows(group, half):
    return group if half == 0 else (4 if group == 0 else 8 - group)


def table_seeds():
    waves = np.zeros((2, 4, 2, 64), np.int64)
    for s in range(2):
        for u in range(4):
            for half in range(2):
                waves[s, u, half] = wave_rows(u, half) + 8 * (64 * s + np.arange(64))
    waves = waves.reshape(1, 1024)
    rows = np.arange(STEPS).reshape(STEPS, 1)
    first = 2.0 * np.pi * ((rows * waves) % NLON) / NLON
    turn = np.broadcast_to(2.0 * np.pi * ((STEPS * waves) % NLON) / NLON, (STEPS, 1024))
    scale = 1.0 / math.sqrt(NLON)
    return np.stack([np.cos(first) * scale, np.sin(first) * scale, np.cos(turn), np.sin(turn)]).astype(np.float32)


def make_table(seeds, table):
    lane = lax.broadcasted_iota(jnp.int32, (STEPS, 128), 1)
    first_half = lane < 64
    for s in range(2):

        def rows(step, carry):
            at = pl.multiple_of(step * STEPS, STEPS)
            after = []
            for u in range(4):
                cosine, sine = carry[u]
                low, high = pl.ds(at, STEPS), pl.ds(at + INNER, STEPS)
                real, imag = pl.ds(s * 256, 128), pl.ds(s * 256 + 128, 128)
                if u == 0:
                    table[u, low, real] = jnp.where(first_half, cosine, 0.0).astype(jnp.bfloat16)
                    table[u, low, imag] = jnp.where(first_half, -sine, 0.0).astype(jnp.bfloat16)
                    table[u, high, real] = jnp.where(first_half, 0.0, cosine).astype(jnp.bfloat16)
                    table[u, high, imag] = jnp.where(first_half, 0.0, -sine).astype(jnp.bfloat16)
                else:
                    table[u, low, real] = cosine.astype(jnp.bfloat16)
                    table[u, low, imag] = (-sine).astype(jnp.bfloat16)
                    table[u, high, real] = jnp.where(first_half, sine, -sine).astype(jnp.bfloat16)
                    table[u, high, imag] = jnp.where(first_half, cosine, -cosine).astype(jnp.bfloat16)
                columns = pl.ds((s * 4 + u) * 128, 128)
                turn_cos, turn_sin = seeds[2, :, columns], seeds[3, :, columns]
                after.append((cosine * turn_cos - sine * turn_sin, sine * turn_cos + cosine * turn_sin))
            return tuple(after)

        start = tuple(
            (seeds[0, :, pl.ds((s * 4 + u) * 128, 128)], seeds[1, :, pl.ds((s * 4 + u) * 128, 128)]) for u in range(4)
        )
        lax.fori_loop(0, INNER // STEPS, rows, start)


def short_transform(grid, left):
    root = math.sqrt(0.5)
    for f in range(2):
        for block in range(3):
            north = [grid[f, 0, :, pl.ds(l * INNER + block * 128, 128)].astype(jnp.float32) for l in range(8)]
            south = [grid[f, 1, :, pl.ds(l * INNER + block * 128, 128)].astype(jnp.float32) for l in range(8)]
            for p in range(2):
                v = [a + b if p == 0 else a - b for a, b in zip(north, south, strict=True)]
                even = [v[l] + v[l + 4] for l in range(4)]
                odd = [v[l] - v[l + 4] for l in range(4)]
                minus = (odd[1] - odd[3]) * root
                plus = (odd[1] + odd[3]) * root
                pieces = (
                    ((even[0] + even[2]) + (even[1] + even[3]), (even[0] + even[2]) - (even[1] + even[3])),
                    (odd[0] + minus, -odd[2] - plus),
                    (even[0] - even[2], even[3] - even[1]),
                    (odd[0] - minus, odd[2] - plus),
                )
                for u in range(4):
                    for part in range(2):
                        left[u, pl.ds(p * 32 + f * 16, 16), pl.ds(part * INNER + block * 128, 128)] = pieces[u][
                            part
                        ].astype(jnp.bfloat16)


def long_transform(left, table, waves):
    for u in range(4):
        product = jnp.dot(left[u], table[u], preferred_element_type=jnp.float32)
        for s in range(2):
            for r in range(2):
                for p in range(2):
                    waves[s, pl.ds(p * 64 + r * 32, 32), pl.ds(u * 128, 128)] = product[
                        p * 32 : p * 32 + 32, (s * 2 + r) * 128 : (s * 2 + r + 1) * 128
                    ].astype(jnp.bfloat16)


def swap_groups(blocks, shifts):
    lane = lax.broadcasted_iota(jnp.int32, blocks[0].shape, 1)
    blocks = list(blocks)
    for place, shift in enumerate(shifts):
        bit = 1 << place
        keep = (lane & shift) == 0
        for i in range(len(blocks)):
            if i & bit == 0:
                a, b = blocks[i], blocks[i + bit]
                blocks[i] = jnp.where(keep, a, pltpu.roll(b, shift, 1))
                blocks[i + bit] = jnp.where(keep, pltpu.roll(a, 128 - shift, 1), b)
    return blocks


def pick_slots(c, slot_rows, waves, one_hot, picked, puts):
    row = lax.broadcasted_iota(jnp.int32, (64, 128), 0) * 8
    for p in (1, 0):
        for h in range(2):
            slots = jnp.broadcast_to(slot_rows[p, c, h : h + 1, :], (64, 128))
            for u in range(4):
                for half in range(2):
                    here = row + wave_rows(u, half)
                    place = (pl.ds(u * 128 + half * 64, 64), pl.ds(h * 128, 128))
                    one_hot[(p, 0, *place)] = jnp.where(here == slots, 1.0, 0.0).astype(jnp.bfloat16)
                    one_hot[(p, 1, *place)] = jnp.where(here == 511 - slots, 1.0, 0.0).astype(jnp.bfloat16)
        for s in range(2):
            picked[p, s] = jnp.dot(
                waves[s, pl.ds(p * 64, 64), :], one_hot[p, s], preferred_element_type=jnp.float32
            )
    for p in (1, 0):
        for h in range(2):
            blocks = [
                picked[p, g // 4, pl.ds((g % 2) * 32 + (g // 2 % 2) * 16, 16), pl.ds(h * 128, 128)] for g in range(8)
            ]
            for k, block in enumerate(swap_groups(blocks, (1, 2, 64))):
                puts[p](h * 8 + k, block.astype(jnp.bfloat16))


def turn_groups(arrived, c, put):
    blocks = [arrived[c * 16 + f].astype(jnp.float32) for f in range(16)]
    for i, block in enumerate(swap_groups(blocks, (4, 8, 16, 32))):
        put(i, block.astype(jnp.bfloat16))


def turn_legendre(legendre, by_j):
    first = lax.broadcasted_iota(jnp.int32, (128, 128), 0) == 0
    for block in range(6):
        at = pl.ds(block * 128, 128)
        for c in range(5):
            if c < 4:
                values = legendre[pl.ds(c * 128, 128), :, at].astype(jnp.float32)
            else:
                values = legendre[pl.ds(512, 1), :, at].astype(jnp.float32)
            for p in range(2):
                piece = values[:, p, :]
                if c == 4:
                    piece = jnp.where(first, jnp.broadcast_to(piece, (128, 128)), 0.0)
                piece = piece.astype(jnp.bfloat16).T
                for k in range(8):
                    row, depth = divmod(block * 8 + k, ZS)
                    to = (depth % 3 * 16 + row * 4 + depth // 3) * 16
                    by_j[p, pl.ds(to, 16), pl.ds(c * 128, 128)] = piece[k * 16 : k * 16 + 16]


def choose_columns(p, wave, products):
    column = lax.broadcasted_iota(jnp.int32, (64, 640), 1)
    first_count = (MM - wave + 1 - p) >> 1
    second_count = (wave + 2 - p) >> 1
    second = jnp.where(column < first_count + second_count, products[64:], 0.0)
    return jnp.where(column < first_count, products[:64], second)


def wrap(at, size):
    return jnp.where(at >= size, at - size, at)


def arrived_at(ref, semaphore):
    pltpu.make_async_copy(ref, ref, semaphore).wait()


def kernel(
    grid_hbm, slot_hbm, seeds_hbm, legendre_hbm, out,
    grid, slot, seeds, legendre, by_j, flipped, total, table, left, waves, one_hot, picked,
    own_column, all_slots, slot_rows, by_fld, from_fld, by_band, from_band, by_fld_late, from_fld_late, by_band_late, rows,
    input_sem, send_list, recv_list, send_lists, recv_lists,
    send_fld, recv_fld, send_band, recv_band, send_fld_late, recv_fld_late, send_band_late, recv_band_late,
):
    band, fld = lax.axis_index("band"), lax.axis_index("fld")
    x, z = band // ZS, band % ZS
    place = z % 3 * 16 + x * 4 + z // 3
    inputs = (
        pltpu.make_async_copy(seeds_hbm, seeds, input_sem.at[0]),
        pltpu.make_async_copy(grid_hbm, grid, input_sem.at[1]),
        pltpu.make_async_copy(legendre_hbm, legendre, input_sem.at[2]),
    )
    own_slot = pltpu.make_async_copy(slot_hbm, slot, input_sem.at[3])
    own_slot.start()

    all_x = [wrap(x + dx, 4) for dx in range(4)]
    all_z = [wrap(z + dz, ZS) for dz in range(ZS)]
    hops = sorted(((min(dx, 4 - dx) + min(dz, ZS - dz), dx, dz) for dx in range(4) for dz in range(ZS)), reverse=True)
    band_peers = [{"band": all_x[dx] * ZS + all_z[dz]} for far, dx, dz in hops if far]
    fld_peers = [{"fld": wrap(fld + d, FLDS)} for d in sorted(range(1, FLDS), key=lambda d: -min(d, FLDS - d))]

    barrier = pltpu.get_barrier_semaphore()
    for to in band_peers:
        pl.semaphore_signal(barrier, inc=1, device_id=to)
    for to in fld_peers:
        pl.semaphore_signal(barrier, inc=1, device_id=to)
    for copy in inputs:
        copy.start()
    own_slot.wait()
    own_column[fld] = jnp.full((1, 128), slot[0], jnp.int32)
    pl.semaphore_wait(barrier, FLDS - 1 + BANDS - 1)

    for to in fld_peers:
        pltpu.make_async_remote_copy(
            own_column.at[fld], own_column.at[fld], send_list, recv_list, device_id=to
        ).start()
    for copy in inputs[:2]:
        copy.wait()
    make_table(seeds, table)
    short_transform(grid, left)
    arrived_at(own_column.at[pl.ds(0, FLDS - 1)], recv_list)

    lane = lax.broadcasted_iota(jnp.int32, (1, 128), 1)
    of_eight, of_sixteen = lane // 64 * 4 + lane % 4, lane // 4 % 16
    column = [own_column[f] for f in range(FLDS)]
    for h in range(2):
        row = jnp.zeros((1, 128), jnp.int32)
        for k in range(8):
            row = row + jnp.where(of_eight == k, column[h * 8 + k], 0)
        all_slots[band, pl.ds(h, 1), :] = row
    row = jnp.zeros((1, 128), jnp.int32)
    for f in range(FLDS):
        row = row + jnp.where(of_sixteen == f, column[f], 0)
    all_slots[band, pl.ds(2, 1), :] = row
    all_slots[band, pl.ds(3, 1), :] = jnp.zeros((1, 128), jnp.int32)

    for to in band_peers:
        pltpu.make_async_remote_copy(
            all_slots.at[band], all_slots.at[band], send_lists, recv_lists, device_id=to
        ).start()
    long_transform(left, table, waves)
    inputs[2].wait()
    turn_legendre(legendre, by_j)
    arrived_at(all_slots.at[pl.ds(0, BANDS - 1)], recv_lists)
    for c in range(3):
        members = [(i // 4) * ZS + (i % 4) * 3 + c for i in range(16)]
        early = jnp.zeros((2, 128), jnp.int32)
        for i in range(16):
            early = early + jnp.where(of_sixteen == i, all_slots[members[i], pl.ds(0, 2), :], 0)
        slot_rows[0, c] = early
        for h in range(2):
            late = jnp.zeros((1, 128), jnp.int32)
            for k in range(8):
                late = late + jnp.where(of_eight == k, all_slots[members[h * 8 + k], pl.ds(2, 1), :], 0)
            slot_rows[1, c, pl.ds(h, 1), :] = late

    def to_fld(source, target, send, recv, step, c):
        for to in fld_peers:
            pltpu.make_async_remote_copy(
                source.at[to["fld"], c], target.at[c * 16 + fld], send, recv.at[step], device_id=to
            ).start()

    far_first = sorted(
        ((min(dx, 4 - dx) + (3 * k + 1 if k < 2 else 11 - 3 * k), k, dx) for k in range(4) for dx in range(4)), reverse=True
    )

    def to_band(step, send):
        c = wrap(z % 3 + step, 3)
        to_z = [wrap(z + step + 3 * k, ZS) for k in range(4)]
        high = [(at - c) // 3 for at in to_z]
        for far, k, dx in far_first:
            act = functools.partial(send, c * 16 + all_x[dx] * 4 + high[k], {"band": all_x[dx] * ZS + to_z[k]})
            if k or dx:
                act()
            elif not isinstance(step, int):
                pl.when(step > 0)(act)
            elif step:
                act()

    def chunk_out(step, carry):
        c = (z + step) % 3

        def put_band(i, block):
            by_band[c * 16 + i] = block

        def put_fld(f, block):
            by_fld[f, c] = block

        pick_slots(c, slot_rows, waves, one_hot, picked, (put_fld, put_band))
        to_band(step, lambda i, to: pltpu.make_async_remote_copy(
            by_band.at[i], from_band.at[place], send_band, recv_band.at[step], device_id=to
        ).start())
        to_fld(by_fld, from_fld, send_fld, recv_fld, step, c)
        from_fld[c * 16 + fld] = by_fld[fld, c]
        return carry

    lax.fori_loop(0, 3, chunk_out, 0)
    from_band[place] = by_band[place]

    def middle_fld(step):
        c = (z + step) % 3

        def put_band_late(i, block):
            by_band_late[c * 16 + i] = block

        arrived_at(from_fld.at[pl.ds(c * 16, FLDS - 1)], recv_fld.at[step])
        turn_groups(from_fld, c, put_band_late)
        to_band(step, lambda i, to: pltpu.make_async_remote_copy(
            by_band_late.at[i], rows.at[0, place], send_band_late, recv_band_late.at[step], device_id=to
        ).start())
        if step == 0:
            rows[0, place] = by_band_late[place]

    def middle_band(step):
        c = (z + 3 - step) % 3

        def put_fld_late(f, block):
            by_fld_late[f, c] = block

        arrived_at(from_band.at[pl.ds(c * 16, 16 if step else 15)], recv_band.at[step])
        turn_groups(from_band, c, put_fld_late)
        to_fld(by_fld_late, from_fld_late, send_fld_late, recv_fld_late, step, c)
        from_fld_late[c * 16 + fld] = by_fld_late[fld, c]

    middle_fld(0)
    middle_fld(1)
    middle_fld(2)
    middle_band(0)
    middle_band(1)
    middle_band(2)

    def add_chunk(p, c, step):
        for half in range(2):
            piece = rows[p, pl.ds(c * 16 + half * 8, 8)].reshape(128, 128)
            flipped[p, :, pl.ds(half * 128, 128)] = piece.T
        deep = pl.ds(pl.multiple_of(c * 256, 256), 256)
        products = jnp.dot(flipped[p], by_j[p, deep, :], preferred_element_type=jnp.float32)
        if step:
            products = total[p] + products
        if step < 2:
            total[p] = products
        else:
            out[p] = choose_columns(p, slot[0], products).astype(jnp.bfloat16).reshape(32, 2, 640)[:, :, :513]

    arrived_at(own_column.at[pl.ds(0, FLDS - 1)], send_list)
    arrived_at(all_slots.at[pl.ds(0, BANDS - 1)], send_lists)
    arrived_at(by_fld.at[pl.ds(0, FLDS - 1)], send_fld)
    arrived_at(by_band.at[pl.ds(0, BANDS - 1)], send_band)
    def last_fld(step):
        c = (z + 3 - step) % 3

        def put_row(i, block):
            rows[1, c * 16 + i] = block

        arrived_at(from_fld_late.at[pl.ds(c * 16, FLDS - 1)], recv_fld_late.at[step])
        turn_groups(from_fld_late, c, put_row)
        add_chunk(1, c, step)

    def last_band(step):
        c = (z + 3 - step) % 3
        arrived_at(rows.at[0, pl.ds(c * 16, 16 if step else 15)], recv_band_late.at[step])
        add_chunk(0, c, step)

    last_fld(0)
    last_band(0)
    last_fld(1)
    last_band(1)
    last_fld(2)
    last_band(2)
    arrived_at(by_fld_late.at[pl.ds(0, FLDS - 1)], send_fld_late)
    arrived_at(by_band_late.at[pl.ds(0, BANDS - 1)], send_band_late)


def spectrum_at_owner(grid_fields, slot_wave, legendre):
    bf16, f32, i32 = jnp.bfloat16, jnp.float32, jnp.int32
    hbm = pl.BlockSpec(memory_space=pltpu.HBM)
    dma = pltpu.SemaphoreType.DMA
    operands = grid_fields, slot_wave, jnp.asarray(table_seeds()), legendre
    return pl.pallas_call(
        kernel,
        out_shape=jax.ShapeDtypeStruct((2, 32, 2, legendre.shape[0]), bf16),
        in_specs=[hbm] * 4,
        out_specs=pl.BlockSpec(memory_space=pltpu.VMEM),
        scratch_shapes=[
            pltpu.VMEM(grid_fields.shape, bf16),
            pltpu.SMEM((2,), i32),
            pltpu.VMEM((4, STEPS, 1024), f32),
            pltpu.VMEM(legendre.shape, bf16),
            pltpu.VMEM((2, 768, 640), bf16),
            pltpu.VMEM((2, 128, 256), bf16),
            pltpu.VMEM((2, 128, 640), f32),
            pltpu.VMEM((4, 768, 512), bf16),
            pltpu.VMEM((4, 64, 768), bf16),
            pltpu.VMEM((2, 128, 512), bf16),
            pltpu.VMEM((2, 2, 512, 256), bf16),
            pltpu.VMEM((2, 2, 64, 256), f32),
            pltpu.VMEM((FLDS, 1, 128), i32),
            pltpu.VMEM((BANDS, 4, 128), i32),
            pltpu.VMEM((2, 3, 2, 128), i32),
            pltpu.VMEM((FLDS, 3, 16, 128), bf16),
            pltpu.VMEM((48, 16, 128), bf16),
            pltpu.VMEM((48, 16, 128), bf16),
            pltpu.VMEM((48, 16, 128), bf16),
            pltpu.VMEM((FLDS, 3, 16, 128), bf16),
            pltpu.VMEM((48, 16, 128), bf16),
            pltpu.VMEM((48, 16, 128), bf16),
            pltpu.VMEM((2, BANDS, 16, 128), bf16),
            dma((4,)), dma, dma, dma, dma,
            dma, dma((3,)), dma, dma((3,)), dma, dma((3,)), dma, dma((3,)),
        ],
        compiler_params=pltpu.CompilerParams(
            collective_id=0, has_side_effects=True, vmem_limit_bytes=24 * 1024 * 1024
        ),
        name="spectrum_at_owner",
    )(*(pltpu.with_memory_space_constraint(a, pltpu.HBM) for a in operands))


def local(grid_fields, legendre, slot_wave):
    return spectrum_at_owner(grid_fields, slot_wave, legendre[0].transpose(2, 0, 1))[None]


def solution(mesh):
    placed = (P("fld", None, "band", None), P(("band", "fld"), None, None, None), P(("band", "fld")))
    return jax.shard_map(
        local,
        mesh=mesh,
        in_specs=placed,
        out_specs=P(("band", "fld"), None, None, None, None),
        check_vma=False,
    )
```
